128 devices in a mesh: sample: 8 (over z_lo, y), feat: 16 (over x, z_hi, core).
Axes of the slice: x: 4, y: 4, z: 4 (z_hi: 2, z_lo: 2; z = z_hi * 2 + z_lo), core: 2. Of those that a mesh axis runs over, the one named last changes fastest.
Arguments:
- view_a: bfloat16 [1024, 16384], P('sample', 'feat'), may hold values from -60 to 60
- view_b: bfloat16 [1024, 16384], P('sample', 'feat'), may hold values from -60 to 60
Outputs:
- loss: float32 [], replicated
- grad_a: bfloat16 [1024, 16384], P('sample', 'feat')
- grad_b: bfloat16 [1024, 16384], P('sample', 'feat')
The draws below stay inside these ranges and needn't reach their ends.
All inputs are finite; a program needn't handle non-finite values.
Results may differ from the reference program's by a relative error of at most 0.02.
Values may be sent and summed in bfloat16 or wider, within the bound.
No kernel may reach another device: no remote copies, remote signals or barrier semaphores. Data moves between devices by JAX's collectives and lax.ppermute only.
A program may use at most 64 MiB of HBM per device.

```python
import math
import jax
import jax.numpy as jnp
from jax import lax

F = 16384
BATCH = 1024
N_SAMPLE = 8
N_FEAT = 16


def pair_views(key):
    subkeys = jax.random.split(jax.random.fold_in(key, 11), 9)
    block_width = F // N_FEAT
    feature_pos = (jnp.arange(F, dtype=jnp.int32) % block_width).astype(jnp.float32) / block_width
    private_a = jax.random.normal(subkeys[0], (BATCH, F), jnp.float32)
    private_b = jax.random.normal(subkeys[1], (BATCH, F), jnp.float32)
    shared_weight = 0.35
    row_top = math.log(3.0)
    mix_top = 0.95
    mix_fall = 0.75
    load_rise = math.log(3.0)
    common_rows = jax.random.normal(subkeys[2], (BATCH, 1), jnp.float32)
    loading = jax.random.normal(subkeys[3], (1, F), jnp.float32) * jnp.exp(load_rise * feature_pos)[None, :]
    row_pos = jnp.arange(BATCH, dtype=jnp.float32) / max(BATCH - 1, 1)
    row_scale = jnp.exp(row_top * row_pos)[:, None] * jax.random.uniform(subkeys[4], (BATCH, 1), jnp.float32, 0.7, 1.4)
    mixing = (mix_top - mix_fall * feature_pos)[None, :] * jax.random.uniform(subkeys[5], (1, F), jnp.float32, 0.75, 1.0)
    scale_a = jnp.exp(jax.random.uniform(subkeys[6], (1, F), jnp.float32, math.log(0.5), math.log(3.0)))
    scale_b = jnp.exp(jax.random.uniform(subkeys[7], (1, F), jnp.float32, math.log(0.5), math.log(3.0)))
    offsets = jax.random.normal(subkeys[8], (2, F), jnp.float32)
    shared = shared_weight * common_rows * loading
    signal_a = private_a + shared
    signal_b = mixing * private_a + jnp.sqrt(1.0 - mixing * mixing) * private_b + shared
    first = jnp.clip(offsets[0][None, :] + scale_a * row_scale * signal_a, -60.0, 60.0)
    second = jnp.clip(offsets[1][None, :] + scale_b * row_scale * signal_b, -60.0, 60.0)
    return (first, second)


def draw_view_a(key, part):
    return pair_views(key)[0].astype(jnp.bfloat16)


def draw_view_b(key, part):
    return pair_views(key)[1].astype(jnp.bfloat16)


def setup_inputs(seed: int = 0) -> dict:
    seeds = jax.random.split(jax.random.key(seed), 3)
    return {
        "view_a": draw_view_a(jax.random.fold_in(seeds[2], 71), 0),
        "view_b": draw_view_b(jax.random.fold_in(seeds[2], 71), 0),
    }


EPSILON = 1e-05
OFF_WEIGHT = 0.0051

def normalize(raw):
    floats = raw.astype(jnp.float32)
    mean_val = lax.optimization_barrier(jnp.mean(floats, axis=0))
    variance = lax.optimization_barrier(jnp.mean(floats * floats, axis=0)) - mean_val * mean_val
    scale_inv = lax.rsqrt(variance + EPSILON)
    return (((floats - mean_val) * scale_inv).astype(jnp.bfloat16), scale_inv)

def backnorm(grad_norm, normed, scale_inv):
    floats = normed.astype(jnp.float32)
    mean_grad = lax.optimization_barrier(jnp.mean(grad_norm, axis=0))
    mean_cross = lax.optimization_barrier(jnp.mean(grad_norm * floats, axis=0))
    return (scale_inv * (grad_norm - mean_grad - floats * mean_cross)).astype(jnp.bfloat16)

def reference(view_a, view_b):
    norm_a, scale_a = normalize(view_a)
    norm_b, scale_b = normalize(view_b)
    total_rows = view_a.shape[0]
    feature_count = view_a.shape[1]
    inv_rows = 1.0 / total_rows
    float_a = norm_a.astype(jnp.float32)
    float_b = norm_b.astype(jnp.float32)
    block_rows = feature_count // N_FEAT
    sub_width = block_rows // N_SAMPLE
    split_b = float_b.reshape(total_rows, N_FEAT, N_SAMPLE, sub_width)
    column_ids = jnp.arange(feature_count, dtype=jnp.int32)

    def block_step(folded, block_id):
        loss_sum, grad_nb = folded
        first_row = (block_id * block_rows).astype(jnp.int32)
        rows_a = lax.dynamic_slice_in_dim(float_a, first_row, block_rows, 1)
        correlation = jnp.dot(rows_a.T, float_b, precision=lax.Precision.HIGHEST) * inv_rows
        row_ids = first_row + jnp.arange(block_rows, dtype=jnp.int32)
        on_diagonal = row_ids[:, None] == column_ids[None, :]
        missing = 1.0 - correlation
        piece_loss = jnp.sum(jnp.where(on_diagonal, missing * missing, OFF_WEIGHT * correlation * correlation))
        factor = jnp.where(on_diagonal, correlation - 1.0, OFF_WEIGHT * correlation).astype(jnp.bfloat16)
        factor_wide = factor.astype(jnp.float32)
        split_factor = factor_wide.reshape(block_rows, N_FEAT, N_SAMPLE, sub_width)
        parts = jnp.einsum('nbsk,rbsk->snr', split_b, split_factor, precision=lax.Precision.HIGHEST)
        grad_block = lax.optimization_barrier(jnp.sum(parts.astype(jnp.bfloat16).astype(jnp.float32), axis=0))
        piece = jnp.dot(rows_a, factor_wide, precision=lax.Precision.HIGHEST)
        grad_nb = grad_nb + piece.astype(jnp.bfloat16).astype(jnp.float32)
        return ((loss_sum + piece_loss, grad_nb), grad_block)
    initial = (jnp.zeros((), jnp.float32), jnp.zeros((total_rows, feature_count), jnp.float32))
    (loss_sum, grad_nb), grad_blocks = lax.scan(block_step, initial, jnp.arange(N_FEAT, dtype=jnp.int32))
    grad_na = jnp.transpose(grad_blocks, (1, 0, 2)).reshape(total_rows, feature_count)
    loss = loss_sum / feature_count
    return (loss, backnorm(grad_na, norm_a, scale_a), backnorm(grad_nb, norm_b, scale_b))
```

```python
import jax
import jax.numpy as jnp
from jax import lax
from jax.sharding import PartitionSpec as P

EPSILON = 1e-05
OFF_WEIGHT = 0.0051


def gather_rows(block, axis):
    members = lax.axis_size(axis)
    copies = jnp.broadcast_to(block[None], (members,) + block.shape)
    copies = copies.reshape((members * block.shape[0],) + block.shape[1:])
    return lax.all_to_all(copies, axis, split_axis=0, concat_axis=0, tiled=True)


def normalize(raw, inv_rows):
    floats = raw.astype(jnp.float32)
    mean = jnp.sum(floats, axis=0) * inv_rows
    variance = jnp.sum(floats * floats, axis=0) * inv_rows - mean * mean
    scale = lax.rsqrt(variance + EPSILON)
    return ((floats - mean) * scale).astype(jnp.bfloat16), mean, scale


def own_rows(view, mean, scale):
    return ((view.astype(jnp.float32) - mean) * scale).astype(jnp.bfloat16)


def gram_rows(own, full, first_row, shift):
    rows = lax.dot_general(own, full, (((1,), (1,)), ((), ())), preferred_element_type=jnp.float32)
    row_ids = first_row + lax.broadcasted_iota(jnp.int32, rows.shape, 0)
    col_ids = lax.broadcasted_iota(jnp.int32, rows.shape, 1)
    return jnp.where(row_ids == col_ids, rows - shift, rows).astype(jnp.bfloat16)


def body(view_a, view_b):
    rows_dev, cols_dev = view_a.shape
    groups = lax.axis_size("sample")
    blocks = lax.axis_size("feat")
    total_rows = rows_dev * groups
    total_cols = cols_dev * blocks
    inv_rows = 1.0 / total_rows
    first_row = lax.axis_index("sample") * rows_dev
    f32 = jnp.float32
    bf16 = jnp.bfloat16

    raw_a = gather_rows(view_a, "sample")
    raw_b = gather_rows(view_b, "sample")
    full_a, mean_a, scale_a = normalize(raw_a, inv_rows)
    full_b, mean_b, scale_b = normalize(raw_b, inv_rows)
    own_a = own_rows(view_a, mean_a, scale_a)
    own_b = own_rows(view_b, mean_b, scale_b)

    part_a = gram_rows(own_a, full_a, first_row, float(cols_dev))
    part_b = gram_rows(own_b, full_b, first_row, float(cols_dev))
    diag = jnp.sum(full_a.astype(f32) * full_b.astype(f32), axis=0) * inv_rows
    slope = (diag - 1.0) - OFF_WEIGHT * diag
    diag_loss = jnp.sum((1.0 - diag) * (1.0 - diag) - OFF_WEIGHT * diag * diag)
    high = diag_loss.astype(bf16)
    low = (diag_loss - high.astype(f32)).astype(bf16)
    lane = lax.broadcasted_iota(jnp.int32, (2 * rows_dev, 128), 1)
    extra = jnp.where(lane == 0, high, jnp.where(lane == 1, low, jnp.zeros((), bf16)))
    payload = jnp.concatenate([jnp.concatenate([part_a, part_b], axis=0), extra], axis=1)
    moved = lax.all_to_all(payload, "feat", split_axis=0, concat_axis=0, tiled=True)
    summed = jnp.sum(moved.reshape(blocks, -1, payload.shape[1]).astype(f32), axis=0)
    diag_total = summed[0, total_rows] + summed[0, total_rows + 1]
    gram = gather_rows(summed[:, :total_rows].astype(bf16), "feat")
    gram_a, gram_b = gram[:rows_dev], gram[rows_dev:]

    factor = OFF_WEIGHT * inv_rows
    shift = factor * total_cols
    norm_a = own_a.astype(f32)
    norm_b = own_b.astype(f32)
    grad_na = (
        factor * jnp.dot(gram_b, full_a, preferred_element_type=f32)
        + shift * norm_a
        + slope * norm_b
    )
    grad_nb = (
        factor * jnp.dot(gram_a, full_b, preferred_element_type=f32)
        + shift * norm_b
        + slope * norm_a
    )

    row_ids = first_row + lax.broadcasted_iota(jnp.int32, gram_a.shape, 0)
    col_ids = lax.broadcasted_iota(jnp.int32, gram_a.shape, 1)
    back = jnp.where(row_ids == col_ids, f32(total_cols), f32(0.0))
    square = jnp.sum((gram_a.astype(f32) + back) * (gram_b.astype(f32) + back))
    stats = jnp.stack(
        [
            jnp.sum(grad_na, axis=0),
            jnp.sum(grad_na * norm_a, axis=0),
            jnp.sum(grad_nb, axis=0),
            jnp.sum(grad_nb * norm_b, axis=0),
            jnp.broadcast_to(square, (cols_dev,)),
        ]
        + [jnp.zeros((cols_dev,), f32)] * 3
    )
    stats = jnp.sum(gather_rows(stats, "sample").reshape(groups, 8, cols_dev), axis=0)
    means = stats[:4] * inv_rows
    grad_a = (scale_a * (grad_na - means[0] - norm_a * means[1])).astype(bf16)
    grad_b = (scale_b * (grad_nb - means[2] - norm_b * means[3])).astype(bf16)
    loss = (diag_total + OFF_WEIGHT * (stats[4, 0] * (inv_rows * inv_rows))) / total_cols
    return (loss, grad_a, grad_b)


def solution(mesh):
    in_specs = (P("sample", "feat"), P("sample", "feat"))
    out_specs = (P(), P("sample", "feat"), P("sample", "feat"))
    return jax.shard_map(body, mesh=mesh, in_specs=in_specs, out_specs=out_specs, check_vma=False)
```

```python
import jax
import jax.numpy as jnp
from jax import lax
from jax.sharding import PartitionSpec as P

EPSILON = 1e-05
OFF_WEIGHT = 0.0051
RING = 4
CORES = 2
F32 = jnp.float32
BF16 = jnp.bfloat16


def send_sample(block, turn, step):
    pairs = lax.axis_size("sample") // RING
    moves = [
        (z * RING + y, (z + turn) % pairs * RING + (y + step) % RING)
        for z in range(pairs)
        for y in range(RING)
    ]
    return lax.ppermute(block, "sample", moves)


def swap_cores(block):
    return lax.ppermute(block, "feat", [(i, i ^ 1) for i in range(lax.axis_size("feat"))])


def exchange_chips(block):
    members = lax.axis_size("feat") // CORES
    groups = [[i * CORES + core for i in range(members)] for core in range(CORES)]
    return lax.all_to_all(
        block, "feat", split_axis=0, concat_axis=0, tiled=True, axis_index_groups=groups
    )


def repeat_block(block, members):
    copies = jnp.broadcast_to(block[None], (members,) + block.shape)
    return copies.reshape((members * block.shape[0],) + block.shape[1:])


def gather_views(a, b):
    rows = a.shape[0]
    half = rows // 2
    b_back = send_sample(b, 0, 1)
    b_on = send_sample(b, 0, -1)
    a_pair = jnp.concatenate([a, send_sample(a, 1, 0)])
    b_far = jnp.concatenate([send_sample(b_back[:half], 0, 1), send_sample(b_on[half:], 0, -1)])
    a_back = send_sample(a_pair, 0, 1)
    a_on = send_sample(a_pair, 0, -1)
    b_over = send_sample(jnp.concatenate([b, b_back, b_on]), 1, 0)
    a_far = send_sample(a_back[:rows], 0, 1)
    a_far_over = send_sample(a_on[rows:], 0, -1)
    b_far_over = send_sample(b_far, 1, 0)
    all_a = [a, a_back[:rows], a_on[:rows], a_far]
    all_a += [a_pair[rows:], a_back[rows:], a_on[rows:], a_far_over]
    all_b = [b, b_back, b_on, b_far, b_over, b_far_over]
    return jnp.concatenate(all_a), jnp.concatenate(all_b)


def normalize(raw, inv_rows):
    floats = raw.astype(F32)
    mean = jnp.sum(floats, axis=0) * inv_rows
    variance = jnp.sum(floats * floats, axis=0) * inv_rows - mean * mean
    scale = lax.rsqrt(variance + EPSILON)
    return ((floats - mean) * scale).astype(BF16), scale


def on_own(rows):
    row_ids = lax.broadcasted_iota(jnp.int32, rows.shape, 0)
    return row_ids == lax.broadcasted_iota(jnp.int32, rows.shape, 1)


def gram_rows(own, full, shift):
    rows = lax.dot_general(own, full, (((1,), (1,)), ((), ())), preferred_element_type=F32)
    return jnp.where(on_own(rows), rows - shift, rows)


def with_scalar(rows, value):
    high = value.astype(BF16)
    low = (value - high.astype(F32)).astype(BF16)
    lane = lax.broadcasted_iota(jnp.int32, (rows.shape[0], 128), 1)
    extra = jnp.where(lane == 0, high, jnp.where(lane == 1, low, jnp.zeros((), BF16)))
    return jnp.concatenate([rows.astype(BF16), extra], axis=1)


def body(view_a, view_b):
    rows_dev, cols_dev = view_a.shape
    groups = lax.axis_size("sample")
    blocks = lax.axis_size("feat")
    chips = blocks // CORES
    total_rows = rows_dev * groups
    total_cols = cols_dev * blocks
    inv_rows = 1.0 / total_rows
    first_core = lax.axis_index("feat") % CORES == 0

    raw_a, raw_b = gather_views(view_a, view_b)
    full_a, scale_a = normalize(raw_a, inv_rows)
    full_b, scale_b = normalize(raw_b, inv_rows)
    own_a = full_a[:rows_dev]
    own_b = full_b[:rows_dev]

    part_a = gram_rows(own_a, full_a, float(cols_dev))
    part_b = gram_rows(own_b, full_b, float(cols_dev))
    diag = jnp.sum(full_a.astype(F32) * full_b.astype(F32), axis=0) * inv_rows
    slope = (diag - 1.0) - OFF_WEIGHT * diag
    diag_loss = jnp.sum((1.0 - diag) * (1.0 - diag) - OFF_WEIGHT * diag * diag)

    other = swap_cores(with_scalar(jnp.where(first_core, part_b, part_a), diag_loss))
    other = other.astype(F32)
    kept = jnp.where(first_core, part_a, part_b) + other[:, :total_rows]
    chip_loss = diag_loss + (other[0, total_rows] + other[0, total_rows + 1])
    moved = exchange_chips(with_scalar(kept, chip_loss))
    summed = jnp.sum(moved.reshape(chips, -1, moved.shape[1]).astype(F32), axis=0)
    diag_total = summed[0, total_rows] + summed[0, total_rows + 1]
    mine = exchange_chips(repeat_block(summed[:, :total_rows].astype(BF16), chips))
    theirs = swap_cores(mine)
    gram_a = jnp.where(first_core, mine, theirs)
    gram_b = jnp.where(first_core, theirs, mine)

    factor = OFF_WEIGHT * inv_rows
    shift = factor * total_cols
    norm_a = own_a.astype(F32)
    norm_b = own_b.astype(F32)
    grad_na = (
        factor * jnp.dot(gram_b, full_a, preferred_element_type=F32)
        + shift * norm_a
        + slope * norm_b
    )
    grad_nb = (
        factor * jnp.dot(gram_a, full_b, preferred_element_type=F32)
        + shift * norm_b
        + slope * norm_a
    )

    back = jnp.where(on_own(gram_a), F32(total_cols), F32(0.0))
    square = jnp.sum((gram_a.astype(F32) + back) * (gram_b.astype(F32) + back))
    stats = jnp.stack(
        [
            jnp.sum(grad_na, axis=0),
            jnp.sum(grad_na * norm_a, axis=0),
            jnp.sum(grad_nb, axis=0),
            jnp.sum(grad_nb * norm_b, axis=0),
            jnp.broadcast_to(square, (cols_dev,)),
        ]
        + [jnp.zeros((cols_dev,), F32)] * 3
    )
    stats = lax.all_to_all(
        repeat_block(stats, groups), "sample", split_axis=0, concat_axis=0, tiled=True
    )
    stats = jnp.sum(stats.reshape(groups, 8, cols_dev), axis=0)
    means = stats[:4] * inv_rows
    grad_a = (scale_a * (grad_na - means[0] - norm_a * means[1])).astype(BF16)
    grad_b = (scale_b * (grad_nb - means[2] - norm_b * means[3])).astype(BF16)
    loss = (diag_total + OFF_WEIGHT * (stats[4, 0] * (inv_rows * inv_rows))) / total_cols
    return (loss, grad_a, grad_b)


def solution(mesh):
    in_specs = (P("sample", "feat"), P("sample", "feat"))
    out_specs = (P(), P("sample", "feat"), P("sample", "feat"))
    return jax.shard_map(body, mesh=mesh, in_specs=in_specs, out_specs=out_specs, check_vma=False)
```

```python
import functools
import jax
import jax.numpy as jnp
from jax import lax
from jax.experimental import pallas as pl
from jax.experimental.pallas import tpu as pltpu
from jax.sharding import PartitionSpec as P

EPSILON = 1e-05
OFF_WEIGHT = 0.0051
RING = 4
CORES = 2
F32 = jnp.float32
BF16 = jnp.bfloat16
LANES = 128


def send_sample(block, turn, step):
    pairs = lax.axis_size("sample") // RING
    moves = [
        (z * RING + y, (z + turn) % pairs * RING + (y + step) % RING)
        for z in range(pairs)
        for y in range(RING)
    ]
    return lax.ppermute(block, "sample", moves)


def swap_cores(block):
    return lax.ppermute(block, "feat", [(i, i ^ 1) for i in range(lax.axis_size("feat"))])


def exchange_chips(block):
    members = lax.axis_size("feat") // CORES
    groups = [[i * CORES + core for i in range(members)] for core in range(CORES)]
    return lax.all_to_all(
        block, "feat", split_axis=0, concat_axis=0, tiled=True, axis_index_groups=groups
    )


def repeat_block(block, members):
    copies = jnp.broadcast_to(block[None], (members,) + block.shape)
    return copies.reshape((members * block.shape[0],) + block.shape[1:])


def gather_views(a, b):
    rows = a.shape[0]
    half = rows // 2
    b_back = send_sample(b, 0, 1)
    b_on = send_sample(b, 0, -1)
    a_pair = jnp.concatenate([a, send_sample(a, 1, 0)])
    b_far = jnp.concatenate([send_sample(b_back[:half], 0, 1), send_sample(b_on[half:], 0, -1)])
    a_back = send_sample(a_pair, 0, 1)
    a_on = send_sample(a_pair, 0, -1)
    b_over = send_sample(jnp.concatenate([b, b_back, b_on]), 1, 0)
    a_far = send_sample(a_back[:rows], 0, 1)
    a_far_over = send_sample(a_on[rows:], 0, -1)
    b_far_over = send_sample(b_far, 1, 0)
    parts_a = [a, a_back, a_on, a_far, a_pair[rows:], a_far_over]
    parts_b = [b, b_back, b_on, b_far, b_over, b_far_over]
    return parts_a, parts_b


def call(kernel, steps, args, outs, scratch=(), limit=16):
    def spec(shape, cut):
        rows, cols = shape
        if cut:
            return pl.BlockSpec((rows, cols // steps), lambda i: (0, i))
        return pl.BlockSpec((rows, cols), lambda i: (0, 0))

    def out_spec(out, cut):
        if out.shape == (1,):
            return pl.BlockSpec(memory_space=pltpu.SMEM)
        return spec(out.shape, cut)

    return pl.pallas_call(
        kernel,
        grid=(steps,),
        out_shape=[out for out, _ in outs],
        in_specs=[pl.BlockSpec(memory_space=pltpu.SMEM)] + [spec(x.shape, c) for x, c in args[1:]],
        out_specs=[out_spec(out, cut) for out, cut in outs],
        scratch_shapes=list(scratch),

    )(*[args[0]] + [x for x, _ in args[1:]])


def on_own(shape):
    row_ids = lax.broadcasted_iota(jnp.int32, shape, 0)
    return row_ids == lax.broadcasted_iota(jnp.int32, shape, 1)


def split_scalar(value, rows):
    wide = jnp.broadcast_to(value, (rows, LANES))
    high = wide.astype(BF16).astype(F32)
    lane = lax.broadcasted_iota(jnp.int32, wide.shape, 1)
    return jnp.where(lane < LANES // 2, high, (wide - high).astype(BF16).astype(F32))


def gram_kernel(core, *refs):
    a, a_back, a_on, a_far, a_over, a_far_over = refs[:6]
    b, b_back, b_on, b_far, b_over, b_far_over = refs[6:12]
    full_a, full_b, vecs, keep, send, part_a, part_b, loss = refs[12:]
    step = pl.program_id(0)
    steps = pl.num_programs(0)
    rows, cols = a.shape
    total_rows = full_a.shape[0]
    inv_rows = 1.0 / total_rows
    top, high = pl.ds(0, rows), pl.ds(rows, rows)
    raw_a = [(a, top), (a_back, top), (a_on, top), (a_far, top)]
    raw_a += [(a_over, top), (a_back, high), (a_on, high), (a_far_over, top)]
    raw_b = [(b, top), (b_back, top), (b_on, top), (b_far, top)]
    raw_b += [(b_over, pl.ds(i * rows, rows)) for i in range(3)] + [(b_far_over, top)]

    @pl.when(step == 0)
    def _():
        part_a[...] = jnp.zeros_like(part_a)
        part_b[...] = jnp.zeros_like(part_b)
        loss[...] = jnp.zeros_like(loss)

    def view(raw, full, part):
        floats = jnp.concatenate([ref[piece, :] for ref, piece in raw]).astype(F32)
        mean = jnp.sum(floats, axis=0, keepdims=True) * inv_rows
        square = jnp.sum(floats * floats, axis=0, keepdims=True) * inv_rows
        scale = lax.rsqrt(square - mean * mean + EPSILON)
        norm = ((floats - mean) * scale).astype(BF16)
        full[...] = norm
        part[...] += lax.dot_general(
            norm[:rows], norm, (((1,), (1,)), ((), ())), preferred_element_type=F32
        )
        return norm, scale

    norm_a, scale_a = view(raw_a, full_a, part_a)
    norm_b, scale_b = view(raw_b, full_b, part_b)
    diag = jnp.sum(norm_a.astype(F32) * norm_b.astype(F32), axis=0, keepdims=True) * inv_rows
    loss[...] += (1.0 - diag) * (1.0 - diag) - OFF_WEIGHT * diag * diag
    slope = (diag - 1.0) - OFF_WEIGHT * diag
    vecs[...] = jnp.concatenate([scale_a, scale_b, slope, jnp.zeros((5, cols), F32)])

    @pl.when(step == steps - 1)
    def _():
        own = on_own(part_a.shape)
        gram_a = part_a[...] - jnp.where(own, 1.0 * cols * steps, 0.0)
        gram_b = part_b[...] - jnp.where(own, 1.0 * cols * steps, 0.0)
        keep[:, total_rows:] = split_scalar(jnp.sum(loss[...], axis=1, keepdims=True), rows)
        send[:, total_rows:] = jnp.zeros((rows, LANES), BF16)

        @pl.when(core[0] == 0)
        def _():
            keep[:, :total_rows] = gram_a
            send[:, :total_rows] = gram_b.astype(BF16)

        @pl.when(core[0] != 0)
        def _():
            keep[:, :total_rows] = gram_b
            send[:, :total_rows] = gram_a.astype(BF16)


def grad_kernel(core, mine, theirs, full_a, full_b, vecs, grad_na, grad_nb, stats, *, total_cols):
    rows, total_rows = mine.shape
    cols = grad_na.shape[1]
    factor = OFF_WEIGHT / total_rows
    shift = factor * total_cols
    first = core[0] == 0
    gram_a = jnp.where(first, mine[...], theirs[...])
    gram_b = jnp.where(first, theirs[...], mine[...])
    norm_a = full_a[:rows, :].astype(F32)
    norm_b = full_b[:rows, :].astype(F32)
    slope = vecs[2:3, :]
    wide_a = jnp.dot(gram_b, full_a[...], preferred_element_type=F32)
    wide_b = jnp.dot(gram_a, full_b[...], preferred_element_type=F32)
    wide_a = factor * wide_a + shift * norm_a + slope * norm_b
    wide_b = factor * wide_b + shift * norm_b + slope * norm_a
    grad_na[...] = wide_a
    grad_nb[...] = wide_b
    sums = [
        jnp.sum(wide_a, axis=0, keepdims=True),
        jnp.sum(wide_a * norm_a, axis=0, keepdims=True),
        jnp.sum(wide_b, axis=0, keepdims=True),
        jnp.sum(wide_b * norm_b, axis=0, keepdims=True),
        jnp.zeros((4, cols), F32),
    ]
    sums = jnp.concatenate(sums)
    copies = stats.shape[0] // 8
    for member in range(copies):
        stats[pl.ds(member * 8, 8), :] = sums

    @pl.when(pl.program_id(0) == 0)
    def _():
        back = jnp.where(on_own(mine.shape), 1.0 * total_cols, 0.0)
        square = (gram_a.astype(F32) + back) * (gram_b.astype(F32) + back)
        square = jnp.sum(jnp.sum(square, axis=0, keepdims=True), axis=1, keepdims=True)
        for member in range(copies):
            stats[pl.ds(member * 8 + 4, 1), :] = jnp.broadcast_to(square, (1, cols))


def out_kernel(
    core, stats, grad_na, grad_nb, own_a, own_b, vecs, diag, grad_a, grad_b, loss, *, total_cols
):
    del core
    members = stats.shape[0] // 8
    inv_rows = 1.0 / (own_a.shape[0] * members)
    sums = stats[0:8, :]
    for member in range(1, members):
        sums += stats[pl.ds(member * 8, 8), :]
    means = sums * inv_rows
    norm_a = own_a[...].astype(F32)
    norm_b = own_b[...].astype(F32)
    wide_a = grad_na[...] - means[0:1] - norm_a * means[1:2]
    wide_b = grad_nb[...] - means[2:3] - norm_b * means[3:4]
    grad_a[...] = (vecs[0:1, :] * wide_a).astype(BF16)
    grad_b[...] = (vecs[1:2, :] * wide_b).astype(BF16)

    @pl.when(pl.program_id(0) == 0)
    def _():
        square = jnp.max(means[4:5, 0:LANES]) * inv_rows
        loss[0] = (jnp.max(diag[0:1, :]) + OFF_WEIGHT * square) / total_cols


def body(view_a, view_b):
    rows, cols = view_a.shape
    groups = lax.axis_size("sample")
    blocks = lax.axis_size("feat")
    chips = blocks // CORES
    total_rows = rows * groups
    total_cols = cols * blocks
    core = (lax.axis_index("feat") & (CORES - 1)).reshape(1)
    shape = jax.ShapeDtypeStruct

    parts_a, parts_b = gather_views(view_a, view_b)
    full_a, full_b, vecs, keep, send = call(
        gram_kernel,
        4,
        [core] + [(part, True) for part in parts_a + parts_b],
        [
            (shape((total_rows, cols), BF16), True),
            (shape((total_rows, cols), BF16), True),
            (shape((8, cols), F32), True),
            (shape((rows, total_rows + LANES), F32), False),
            (shape((rows, total_rows + LANES), BF16), False),
        ],
        [
            pltpu.VMEM((rows, total_rows), F32),
            pltpu.VMEM((rows, total_rows), F32),
            pltpu.VMEM((1, cols // 4), F32),
        ],
        limit=24,
    )
    total = (keep + swap_cores(send).astype(F32)).astype(BF16)
    moved = exchange_chips(total)
    summed = jnp.sum(moved.reshape(chips, -1, moved.shape[1]).astype(F32), axis=0)
    mine = exchange_chips(repeat_block(summed[:, :total_rows].astype(BF16), chips))
    diag = jnp.sum(summed[:8, total_rows:], axis=1, keepdims=True) * (2.0 / LANES)
    diag = jnp.broadcast_to(diag, (8, LANES))
    diag = diag + swap_cores(diag)
    theirs = swap_cores(mine)
    grad_na, grad_nb, stats = call(
        functools.partial(grad_kernel, total_cols=total_cols),
        2,
        [core, (mine, False), (theirs, False), (full_a, True), (full_b, True), (vecs, True)],
        [
            (shape((rows, cols), F32), True),
            (shape((rows, cols), F32), True),
            (shape((groups * 8, cols), F32), True),
        ],
    )
    stats = lax.all_to_all(stats, "sample", split_axis=0, concat_axis=0, tiled=True)
    own = [(full_a[:rows], True), (full_b[:rows], True)]
    grad_a, grad_b, loss = call(
        functools.partial(out_kernel, total_cols=total_cols),
        2,
        [core, (stats, True), (grad_na, True), (grad_nb, True)] + own + [(vecs, True), (diag, False)],
        [
            (shape((rows, cols), BF16), True),
            (shape((rows, cols), BF16), True),
            (shape((1,), F32), False),
        ],
    )
    return (loss.reshape(()), grad_a, grad_b)


def solution(mesh):
    in_specs = (P("sample", "feat"), P("sample", "feat"))
    out_specs = (P(), P("sample", "feat"), P("sample", "feat"))
    return jax.shard_map(body, mesh=mesh, in_specs=in_specs, out_specs=out_specs, check_vma=False)
```

```python
import functools
import jax
import jax.numpy as jnp
from jax import lax
from jax.experimental import pallas as pl
from jax.experimental.pallas import tpu as pltpu
from jax.sharding import PartitionSpec as P

EPSILON = 1e-05
OFF_WEIGHT = 0.0051
RING = 4
CORES = 2
F32 = jnp.float32
BF16 = jnp.bfloat16
LANES = 128


def send_sample(block, turn, step):
    pairs = lax.axis_size("sample") // RING
    moves = [
        (z * RING + y, (z + turn) % pairs * RING + (y + step) % RING)
        for z in range(pairs)
        for y in range(RING)
    ]
    return lax.ppermute(block, "sample", moves)


def swap_cores(block):
    return lax.ppermute(block, "feat", [(i, i ^ 1) for i in range(lax.axis_size("feat"))])


def exchange_chips(block):
    members = lax.axis_size("feat") // CORES
    groups = [[i * CORES + core for i in range(members)] for core in range(CORES)]
    return lax.all_to_all(
        block, "feat", split_axis=0, concat_axis=0, tiled=True, axis_index_groups=groups
    )


def repeat_block(block, members):
    copies = jnp.broadcast_to(block[None], (members,) + block.shape)
    return copies.reshape((members * block.shape[0],) + block.shape[1:])


def after(block, *others):
    return lax.optimization_barrier((block,) + others)[0]


def call(kernel, steps, args, outs, scratch=()):
    def spec(shape, cut, rows=None):
        rows, cols = rows or shape[0], shape[1]
        if cut:
            return pl.BlockSpec((rows, cols // steps), lambda i: (0, i))
        return pl.BlockSpec((rows, cols), lambda i: (0, 0))

    def out_spec(out, cut):
        if out.shape == (1,):
            return pl.BlockSpec(memory_space=pltpu.SMEM)
        return spec(out.shape, cut)

    return pl.pallas_call(
        kernel,
        grid=(steps,),
        out_shape=[out for out, _ in outs],
        in_specs=[pl.BlockSpec(memory_space=pltpu.SMEM)] + [
            spec(arg[0].shape, *arg[1:]) for arg in args[1:]
        ],
        out_specs=[out_spec(out, cut) for out, cut in outs],
        scratch_shapes=list(scratch),

    )(args[0], *[arg[0] for arg in args[1:]])


def on_own(shape):
    row_ids = lax.broadcasted_iota(jnp.int32, shape, 0)
    return row_ids == lax.broadcasted_iota(jnp.int32, shape, 1)


def split_scalar(value, rows):
    wide = jnp.broadcast_to(value, (rows, LANES))
    high = wide.astype(BF16).astype(F32)
    lane = lax.broadcasted_iota(jnp.int32, wide.shape, 1)
    return jnp.where(lane < LANES // 2, high, (wide - high).astype(BF16).astype(F32))


def normalize(pieces, full, part):
    rows = part.shape[0]
    inv_rows = 1.0 / full.shape[0]
    floats = jnp.concatenate(pieces).astype(F32)
    mean = jnp.sum(floats, axis=0, keepdims=True) * inv_rows
    square = jnp.sum(floats * floats, axis=0, keepdims=True) * inv_rows
    scale = lax.rsqrt(square - mean * mean + EPSILON)
    norm = ((floats - mean) * scale).astype(BF16)
    full[...] = norm
    part[...] += lax.dot_general(
        norm[:rows], norm, (((1,), (1,)), ((), ())), preferred_element_type=F32
    )
    return norm, scale


def share_rows(core, part, cols, keep, send):
    rows, total_rows = part.shape
    half = rows // CORES
    gram = part[...] - jnp.where(on_own(part.shape), 1.0 * cols, 0.0)

    @pl.when(core[0] == 0)
    def _():
        keep[:, :total_rows] = gram[:half]
        send[:, :total_rows] = gram[half:].astype(BF16)

    @pl.when(core[0] != 0)
    def _():
        keep[:, :total_rows] = gram[half:]
        send[:, :total_rows] = gram[:half].astype(BF16)


def gram_a_kernel(core, *refs):
    full, scale_ref, keep, send, part = refs[8:]
    step = pl.program_id(0)

    @pl.when(step == 0)
    def _():
        part[...] = jnp.zeros_like(part)

    _, scale = normalize([ref[...] for ref in refs[:8]], full, part)
    scale_ref[...] = jnp.broadcast_to(scale, scale_ref.shape)

    @pl.when(step == pl.num_programs(0) - 1)
    def _():
        share_rows(core, part, full.shape[1] * pl.num_programs(0), keep, send)


def gram_b_kernel(core, *refs):
    b, b_back, b_on, b_far, b_over, b_over_far, full_a = refs[:7]
    full, vecs, keep, send, part, loss = refs[7:]
    step = pl.program_id(0)
    rows, cols = b.shape
    half, total_rows = keep.shape[0], full.shape[0]

    @pl.when(step == 0)
    def _():
        part[...] = jnp.zeros_like(part)
        loss[...] = jnp.zeros_like(loss)

    pieces = [b[...], b_back[:rows, :], b_on[:rows, :], b_far[...]]
    pieces += [b_over[...], b_back[rows:, :], b_on[rows:, :], b_over_far[...]]
    norm, scale = normalize(pieces, full, part)
    diag = jnp.sum(full_a[...].astype(F32) * norm.astype(F32), axis=0, keepdims=True)
    diag = diag * (1.0 / total_rows)
    loss[...] += (1.0 - diag) * (1.0 - diag) - OFF_WEIGHT * diag * diag
    slope = (diag - 1.0) - OFF_WEIGHT * diag
    vecs[...] = jnp.concatenate([scale, slope, jnp.zeros((6, cols), F32)])

    @pl.when(step == pl.num_programs(0) - 1)
    def _():
        share_rows(core, part, cols * pl.num_programs(0), keep, send)
        keep[:, total_rows:] = split_scalar(jnp.sum(loss[...], axis=1, keepdims=True), half)
        send[:, total_rows:] = jnp.zeros((half, LANES), BF16)


def join_rows(core, mine, theirs):
    first = core[0] == 0
    low = jnp.where(first, mine[...], theirs[...])
    return jnp.concatenate([low, jnp.where(first, theirs[...], mine[...])])


def grad_kernel(core, mine, theirs, full, other, vecs, *refs, total_cols, squared):
    grad, stats = refs[-2:]
    total_rows = full.shape[0]
    cols = grad.shape[1]
    factor = OFF_WEIGHT / total_rows
    gram = join_rows(core, mine, theirs)
    rows = gram.shape[0]
    norm = full[:rows, :].astype(F32)
    wide = jnp.dot(gram, full[...], preferred_element_type=F32)
    wide = factor * wide + factor * total_cols * norm + vecs[1:2, :] * other[...].astype(F32)
    grad[...] = wide
    sums = jnp.concatenate(
        [
            jnp.sum(wide, axis=0, keepdims=True),
            jnp.sum(wide * norm, axis=0, keepdims=True),
            jnp.zeros((6, cols), F32),
        ]
    )
    copies = stats.shape[0] // 8
    for member in range(copies):
        stats[pl.ds(member * 8, 8), :] = sums

    if squared:

        @pl.when(pl.program_id(0) == 0)
        def _():
            back = jnp.where(on_own(gram.shape), 1.0 * total_cols, 0.0)
            second = join_rows(core, refs[0], refs[1])
            square = (gram.astype(F32) + back) * (second.astype(F32) + back)
            square = jnp.sum(jnp.sum(square, axis=0, keepdims=True), axis=1, keepdims=True)
            for member in range(copies):
                stats[pl.ds(member * 8 + 2, 1), :] = jnp.broadcast_to(square, (1, cols))


def out_kernel(core, stats, grad, own, scale, *refs, total_cols, with_loss):
    del core
    members = stats.shape[0] // 8
    inv_rows = 1.0 / (own.shape[0] * members)
    sums = stats[0:8, :]
    for member in range(1, members):
        sums += stats[pl.ds(member * 8, 8), :]
    means = sums * inv_rows
    wide = grad[...] - means[0:1] - own[...].astype(F32) * means[1:2]
    refs[-2 if with_loss else -1][...] = (scale[0:1, :] * wide).astype(BF16)

    if with_loss:
        diag, loss = refs[0], refs[-1]

        @pl.when(pl.program_id(0) == 0)
        def _():
            square = jnp.max(means[2:3, 0:LANES]) * inv_rows
            loss[0] = (jnp.max(diag[0:1, :]) + OFF_WEIGHT * square) / total_cols


def add_cores(keep, send):
    return (keep + swap_cores(send).astype(F32)).astype(BF16)


def add_chips(total):
    moved = exchange_chips(total)
    members = lax.axis_size("feat") // CORES
    return jnp.sum(moved.reshape(members, -1, moved.shape[1]).astype(F32), axis=0)


def share_sums(summed):
    members = lax.axis_size("feat") // CORES
    mine = exchange_chips(repeat_block(summed.astype(BF16), members))
    return mine, swap_cores(mine)


def body(view_a, view_b):
    rows, cols = view_a.shape
    groups = lax.axis_size("sample")
    blocks = lax.axis_size("feat")
    half = rows // CORES
    total_rows = rows * groups
    total_cols = cols * blocks
    core = (lax.axis_index("feat") & (CORES - 1)).reshape(1)
    shape = jax.ShapeDtypeStruct
    wide = total_rows + LANES

    a_over = send_sample(view_a, 1, 0)
    a_back = send_sample(view_a, 0, 1)
    a_on = send_sample(view_a, 0, -1)
    b_over = send_sample(after(view_b, a_back, a_on, a_over), 1, 0)
    a_far = send_sample(a_back, 0, 1)
    a_pass = after(a_over, a_back, a_on)
    a_over_back = send_sample(a_pass, 0, 1)
    a_over_on = send_sample(a_pass, 0, -1)
    a_over_far = send_sample(a_over_on, 0, -1)
    b_pair = after(jnp.concatenate([view_b, b_over]), a_over_back, a_over_on)
    b_back = send_sample(b_pair, 0, 1)
    b_on = send_sample(b_pair, 0, -1)
    parts_a = [view_a, a_back, a_on, a_far, a_over, a_over_back, a_over_on, a_over_far]
    full_a, scale_a, keep_a, send_a = call(
        gram_a_kernel,
        4,
        [core] + [(part, True) for part in parts_a],
        [
            (shape((total_rows, cols), BF16), True),
            (shape((8, cols), F32), True),
            (shape((half, total_rows), F32), False),
            (shape((half, total_rows), BF16), False),
        ],
        [pltpu.VMEM((rows, total_rows), F32)],
    )
    total_a = add_cores(keep_a, send_a)
    b_far = send_sample(after(b_back[:rows], total_a), 0, 1)
    b_over_far = send_sample(after(b_on[rows:], total_a), 0, -1)
    summed_a = add_chips(after(total_a, b_back, b_on))
    parts_b = [view_b, b_back, b_on, b_far, after(b_over, summed_a), b_over_far]
    a_mine, a_theirs = share_sums(summed_a)
    full_b, vecs, keep_b, send_b = call(
        gram_b_kernel,
        4,
        [core] + [(part, True) for part in parts_b] + [(full_a, True)],
        [
            (shape((total_rows, cols), BF16), True),
            (shape((8, cols), F32), True),
            (shape((half, wide), F32), False),
            (shape((half, wide), BF16), False),
        ],
        [pltpu.VMEM((rows, total_rows), F32), pltpu.VMEM((1, cols // 4), F32)],
    )
    summed_b = add_chips(add_cores(keep_b, send_b))
    b_mine, b_theirs = share_sums(summed_b[:, :total_rows])
    diag = jnp.sum(summed_b[:, total_rows:], axis=1, keepdims=True) * (2.0 / LANES)
    diag = jnp.broadcast_to(diag, (diag.shape[0], LANES))
    diag = diag + swap_cores(diag)

    def gradient(mine, theirs, full, other, extra):
        grad, stats = call(
            functools.partial(grad_kernel, total_cols=total_cols, squared=bool(extra)),
            2,
            [core, (mine, False), (theirs, False), (full, True), (other, True, rows), (vecs, True)]
            + extra,
            [(shape((rows, cols), F32), True), (shape((groups * 8, cols), F32), True)],
        )
        stats = lax.all_to_all(stats, "sample", split_axis=0, concat_axis=0, tiled=True)
        return grad, stats

    def output(stats, grad, full, scale, extra):
        return call(
            functools.partial(out_kernel, total_cols=total_cols, with_loss=bool(extra)),
            2,
            [core, (stats, True), (grad, True), (full, True, rows), (scale, True)] + extra,
            [(shape((rows, cols), BF16), True)] + [(shape((1,), F32), False)] * len(extra),
        )

    raw_b, stats_b = gradient(a_mine, a_theirs, full_b, full_a, [])
    raw_a, stats_a = gradient(
        b_mine, b_theirs, full_a, full_b, [(a_mine, False), (a_theirs, False)]
    )
    (grad_b,) = output(stats_b, raw_b, full_b, vecs, [])
    grad_a, loss = output(stats_a, raw_a, full_a, scale_a, [(diag, False)])
    return (loss.reshape(()), grad_a, grad_b)


def solution(mesh):
    in_specs = (P("sample", "feat"), P("sample", "feat"))
    out_specs = (P(), P("sample", "feat"), P("sample", "feat"))
    return jax.shard_map(body, mesh=mesh, in_specs=in_specs, out_specs=out_specs, check_vma=False)
```

```python
import functools
import jax
import jax.numpy as jnp
from jax import lax
from jax.experimental import pallas as pl
from jax.experimental.pallas import tpu as pltpu
from jax.sharding import PartitionSpec as P

EPSILON = 1e-05
OFF_WEIGHT = 0.0051
RING = 4
CORES = 2
F32 = jnp.float32
BF16 = jnp.bfloat16
LANES = 128


def send_sample(block, turn, step):
    pairs = lax.axis_size("sample") // RING
    moves = [
        (z * RING + y, (z + turn) % pairs * RING + (y + step) % RING)
        for z in range(pairs)
        for y in range(RING)
    ]
    return lax.ppermute(block, "sample", moves)


def swap_cores(block):
    return lax.ppermute(block, "feat", [(i, i ^ 1) for i in range(lax.axis_size("feat"))])


def exchange_chips(block):
    members = lax.axis_size("feat") // CORES
    groups = [[i * CORES + core for i in range(members)] for core in range(CORES)]
    return lax.all_to_all(
        block, "feat", split_axis=0, concat_axis=0, tiled=True, axis_index_groups=groups
    )


def repeat_block(block, members):
    copies = jnp.broadcast_to(block[None], (members,) + block.shape)
    return copies.reshape((members * block.shape[0],) + block.shape[1:])


def gather_views(a, b):
    rows = a.shape[0]
    half = rows // 2
    b_back = send_sample(b, 0, 1)
    b_on = send_sample(b, 0, -1)
    a_pair = jnp.concatenate([a, send_sample(a, 1, 0)])
    b_far = jnp.concatenate([send_sample(b_back[:half], 0, 1), send_sample(b_on[half:], 0, -1)])
    a_back = send_sample(a_pair, 0, 1)
    a_on = send_sample(a_pair, 0, -1)
    b_over = send_sample(jnp.concatenate([b, b_back, b_on]), 1, 0)
    a_far = send_sample(a_back[:rows], 0, 1)
    a_far_over = send_sample(a_on[rows:], 0, -1)
    b_far_over = send_sample(b_far, 1, 0)
    parts = [a_pair, a_back, a_on, a_far, a_far_over, b, b_back, b_on, b_far, b_over, b_far_over]
    where_a = [(0, 0), (1, 0), (2, 0), (3, 0), (0, 1), (1, 1), (2, 1), (4, 0)]
    where_b = [(5, 0), (6, 0), (7, 0), (8, 0), (9, 0), (9, 1), (9, 2), (10, 0)]
    return parts, *[[(i, j * rows) for i, j in where] for where in (where_a, where_b)]


def call(kernel, steps, args, outs, scratch=(), aliases=None, limit=None):
    def spec(shape, cut, rows=None):
        rows, cols = rows or shape[0], shape[1]
        if cut:
            return pl.BlockSpec((rows, cols // steps), lambda i: (0, i))
        return pl.BlockSpec((rows, cols), lambda i: (0, 0))

    def out_spec(out, cut):
        if out.shape == (1,):
            return pl.BlockSpec(memory_space=pltpu.SMEM)
        return spec(out.shape, cut)

    return pl.pallas_call(
        kernel,
        grid=(steps,),
        out_shape=[out for out, _ in outs],
        in_specs=[pl.BlockSpec(memory_space=pltpu.SMEM)] + [
            spec(arg[0].shape, *arg[1:]) for arg in args[1:]
        ],
        out_specs=[out_spec(out, cut) for out, cut in outs],
        scratch_shapes=list(scratch),
        input_output_aliases=aliases or {},
        compiler_params=pltpu.CompilerParams(vmem_limit_bytes=limit and limit << 20),

    )(args[0], *[arg[0] for arg in args[1:]])


def on_own(shape):
    row_ids = lax.broadcasted_iota(jnp.int32, shape, 0)
    return row_ids == lax.broadcasted_iota(jnp.int32, shape, 1)


def split_scalar(value, rows):
    wide = jnp.broadcast_to(value, (rows, LANES))
    high = wide.astype(BF16).astype(F32)
    lane = lax.broadcasted_iota(jnp.int32, wide.shape, 1)
    return jnp.where(lane < LANES // 2, high, (wide - high).astype(BF16).astype(F32))


def gram_kernel(core, *refs, where_a, where_b):
    vecs, keep, send, part_a, part_b, loss = refs[-6:]
    count = (len(refs) - 6) // 2
    blocks, norms = refs[:count], refs[count : 2 * count]
    step = pl.program_id(0)
    steps = pl.num_programs(0)
    cols = vecs.shape[1]
    rows, total_rows = part_a.shape
    inv_rows = 1.0 / total_rows

    @pl.when(step == 0)
    def _():
        part_a[...] = jnp.zeros_like(part_a)
        part_b[...] = jnp.zeros_like(part_b)
        loss[...] = jnp.zeros_like(loss)

    def view(where, part):
        floats = jnp.concatenate([blocks[i][pl.ds(first, rows), :] for i, first in where])
        floats = floats.astype(F32)
        mean = jnp.sum(floats, axis=0, keepdims=True) * inv_rows
        square = jnp.sum(floats * floats, axis=0, keepdims=True) * inv_rows
        scale = lax.rsqrt(square - mean * mean + EPSILON)
        norm = ((floats - mean) * scale).astype(BF16)
        for place, (i, first) in enumerate(where):
            norms[i][pl.ds(first, rows), :] = norm[place * rows : (place + 1) * rows]
        part[...] += lax.dot_general(
            norm[:rows], norm, (((1,), (1,)), ((), ())), preferred_element_type=F32
        )
        return norm, scale

    norm_a, scale_a = view(where_a, part_a)
    norm_b, scale_b = view(where_b, part_b)
    diag = jnp.sum(norm_a.astype(F32) * norm_b.astype(F32), axis=0, keepdims=True) * inv_rows
    loss[...] += (1.0 - diag) * (1.0 - diag) - OFF_WEIGHT * diag * diag
    slope = (diag - 1.0) - OFF_WEIGHT * diag
    vecs[...] = jnp.concatenate([scale_a, scale_b, slope, jnp.zeros((5, cols), F32)])

    @pl.when(step == steps - 1)
    def _():
        own = on_own(part_a.shape)
        gram_a = part_a[...] - jnp.where(own, 1.0 * cols * steps, 0.0)
        gram_b = part_b[...] - jnp.where(own, 1.0 * cols * steps, 0.0)
        keep[:, total_rows:] = split_scalar(jnp.sum(loss[...], axis=1, keepdims=True), rows)
        send[:, total_rows:] = jnp.zeros((rows, LANES), BF16)

        @pl.when(core[0] == 0)
        def _():
            keep[:, :total_rows] = gram_a
            send[:, :total_rows] = gram_b.astype(BF16)

        @pl.when(core[0] != 0)
        def _():
            keep[:, :total_rows] = gram_b
            send[:, :total_rows] = gram_a.astype(BF16)


def grad_kernel(core, mine, theirs, vecs, *refs, where_a, where_b, total_cols):
    blocks = refs[:-3]
    grad_na, grad_nb, stats = refs[-3:]
    rows, total_rows = mine.shape
    cols = grad_na.shape[1]
    factor = OFF_WEIGHT / total_rows
    shift = factor * total_cols
    first = core[0] == 0
    gram_a = jnp.where(first, mine[...], theirs[...])
    gram_b = jnp.where(first, theirs[...], mine[...])

    def view(where):
        return jnp.concatenate([blocks[i][pl.ds(first, rows), :] for i, first in where])

    full_a, full_b = view(where_a), view(where_b)
    norm_a = full_a[:rows].astype(F32)
    norm_b = full_b[:rows].astype(F32)
    slope = vecs[2:3, :]
    wide_a = jnp.dot(gram_b, full_a, preferred_element_type=F32)
    wide_b = jnp.dot(gram_a, full_b, preferred_element_type=F32)
    wide_a = factor * wide_a + shift * norm_a + slope * norm_b
    wide_b = factor * wide_b + shift * norm_b + slope * norm_a
    grad_na[...] = wide_a
    grad_nb[...] = wide_b
    sums = [
        jnp.sum(wide_a, axis=0, keepdims=True),
        jnp.sum(wide_a * norm_a, axis=0, keepdims=True),
        jnp.sum(wide_b, axis=0, keepdims=True),
        jnp.sum(wide_b * norm_b, axis=0, keepdims=True),
        jnp.zeros((4, cols), F32),
    ]
    sums = jnp.concatenate(sums)
    copies = stats.shape[0] // 8
    for member in range(copies):
        stats[pl.ds(member * 8, 8), :] = sums

    @pl.when(pl.program_id(0) == 0)
    def _():
        back = jnp.where(on_own(mine.shape), 1.0 * total_cols, 0.0)
        square = (gram_a.astype(F32) + back) * (gram_b.astype(F32) + back)
        square = jnp.sum(jnp.sum(square, axis=0, keepdims=True), axis=1, keepdims=True)
        for member in range(copies):
            stats[pl.ds(member * 8 + 4, 1), :] = jnp.broadcast_to(square, (1, cols))


def out_kernel(
    core, stats, grad_na, grad_nb, own_a, own_b, vecs, diag, grad_a, grad_b, loss, *, total_cols
):
    del core
    members = stats.shape[0] // 8
    inv_rows = 1.0 / (own_a.shape[0] * members)
    sums = stats[0:8, :]
    for member in range(1, members):
        sums += stats[pl.ds(member * 8, 8), :]
    means = sums * inv_rows
    norm_a = own_a[...].astype(F32)
    norm_b = own_b[...].astype(F32)
    wide_a = grad_na[...] - means[0:1] - norm_a * means[1:2]
    wide_b = grad_nb[...] - means[2:3] - norm_b * means[3:4]
    grad_a[...] = (vecs[0:1, :] * wide_a).astype(BF16)
    grad_b[...] = (vecs[1:2, :] * wide_b).astype(BF16)

    @pl.when(pl.program_id(0) == 0)
    def _():
        square = jnp.max(means[4:5, 0:LANES]) * inv_rows
        loss[0] = (jnp.max(diag[0:1, :]) + OFF_WEIGHT * square) / total_cols


def body(view_a, view_b):
    rows, cols = view_a.shape
    groups = lax.axis_size("sample")
    blocks = lax.axis_size("feat")
    chips = blocks // CORES
    total_rows = rows * groups
    total_cols = cols * blocks
    core = (lax.axis_index("feat") & (CORES - 1)).reshape(1)
    shape = jax.ShapeDtypeStruct

    parts, where_a, where_b = gather_views(view_a, view_b)
    *norms, vecs, keep, send = call(
        functools.partial(gram_kernel, where_a=where_a, where_b=where_b),
        2,
        [core] + [(part, True) for part in parts],
        [(shape(part.shape, BF16), True) for part in parts]
        + [
            (shape((8, cols), F32), True),
            (shape((rows, total_rows + LANES), F32), False),
            (shape((rows, total_rows + LANES), BF16), False),
        ],
        [
            pltpu.VMEM((rows, total_rows), F32),
            pltpu.VMEM((rows, total_rows), F32),
            pltpu.VMEM((1, cols // 2), F32),
        ],
        aliases={i + 1: i for i in range(len(parts))},
        limit=20,
    )
    total = (keep + swap_cores(send).astype(F32)).astype(BF16)
    moved = exchange_chips(total)
    summed = jnp.sum(moved.reshape(chips, -1, moved.shape[1]).astype(F32), axis=0)
    mine = exchange_chips(repeat_block(summed[:, :total_rows].astype(BF16), chips))
    diag = jnp.sum(summed[:8, total_rows:], axis=1, keepdims=True) * (2.0 / LANES)
    diag = jnp.broadcast_to(diag, (8, LANES))
    diag = diag + swap_cores(diag)
    theirs = swap_cores(mine)
    grad_na, grad_nb, stats = call(
        functools.partial(
            grad_kernel, where_a=where_a, where_b=where_b, total_cols=total_cols
        ),
        1,
        [core, (mine, False), (theirs, False), (vecs, True)] + [(norm, True) for norm in norms],
        [
            (shape((rows, cols), F32), True),
            (shape((rows, cols), F32), True),
            (shape((groups * 8, cols), F32), True),
        ],
        limit=16,
    )
    stats = lax.all_to_all(stats, "sample", split_axis=0, concat_axis=0, tiled=True)
    own = [(norms[where[0][0]], True, rows) for where in (where_a, where_b)]
    grad_a, grad_b, loss = call(
        functools.partial(out_kernel, total_cols=total_cols),
        1,
        [core, (stats, True), (grad_na, True), (grad_nb, True)] + own + [(vecs, True), (diag, False)],
        [
            (shape((rows, cols), BF16), True),
            (shape((rows, cols), BF16), True),
            (shape((1,), F32), False),
        ],
        limit=10,
    )
    return (loss.reshape(()), grad_a, grad_b)


def solution(mesh):
    in_specs = (P("sample", "feat"), P("sample", "feat"))
    out_specs = (P(), P("sample", "feat"), P("sample", "feat"))
    return jax.shard_map(body, mesh=mesh, in_specs=in_specs, out_specs=out_specs, check_vma=False)
```

```python
import functools
import jax
import jax.numpy as jnp
from jax import lax
from jax.experimental import pallas as pl
from jax.experimental.pallas import tpu as pltpu
from jax.sharding import PartitionSpec as P

EPSILON = 1e-05
OFF_WEIGHT = 0.0051
RING = 4
CORES = 2
F32 = jnp.float32
BF16 = jnp.bfloat16
LANES = 128
SUMS = 4
CHUNK = 512


def send_sample(block, turn, step):
    pairs = lax.axis_size("sample") // RING
    moves = [
        (z * RING + y, (z + turn) % pairs * RING + (y + step) % RING)
        for z in range(pairs)
        for y in range(RING)
    ]
    return lax.ppermute(block, "sample", moves)


def swap_cores(block):
    return lax.ppermute(block, "feat", [(i, i ^ 1) for i in range(lax.axis_size("feat"))])


def exchange_chips(block):
    members = lax.axis_size("feat") // CORES
    groups = [[i * CORES + core for i in range(members)] for core in range(CORES)]
    return lax.all_to_all(
        block, "feat", split_axis=0, concat_axis=0, tiled=True, axis_index_groups=groups
    )


def repeat_block(block, members):
    copies = jnp.broadcast_to(block[None], (members,) + block.shape)
    return copies.reshape((members * block.shape[0],) + block.shape[1:])


def call(kernel, args, outs, scratch=(), aliases=None, limit=16):
    def spec(shape):
        return pl.BlockSpec(memory_space=pltpu.SMEM if shape == (1,) else pltpu.VMEM)

    return pl.pallas_call(
        kernel,
        out_shape=outs,
        in_specs=[spec(arg.shape) for arg in args],
        out_specs=[spec(out.shape) for out in outs],
        scratch_shapes=list(scratch),
        input_output_aliases=aliases or {},
        compiler_params=pltpu.CompilerParams(vmem_limit_bytes=limit << 20),
    )(*args)


def bring_kernel(*refs):
    for source, place in zip(refs[: len(refs) // 2], refs[len(refs) // 2 :]):
        place[...] = source[...]


def bring(*blocks):
    return call(bring_kernel, blocks, [jax.ShapeDtypeStruct(x.shape, x.dtype) for x in blocks])


def after(block, *others):
    return lax.optimization_barrier((block,) + others)[0]


def gather_views(a, b):
    rows = a.shape[0]
    b_back = send_sample(b, 0, 1)
    b_on = send_sample(b, 0, -1)
    a_over = send_sample(a, 1, 0)
    a_next = after(a, b_back, b_on, a_over)
    b_far = send_sample(after(b_on, a_over, b_back), 0, -1)
    b_over = send_sample(after(b, a_over, b_back, b_on), 1, 0)
    b_back_over = send_sample(b_back, 1, 0)
    b_on_over = send_sample(b_on, 1, 0)
    a_over_back = send_sample(after(a_over, b_back, b_on), 0, 1)
    a_back = send_sample(a_next, 0, 1)
    a_over_on = send_sample(after(a_over, b_back, b_on), 0, -1)
    a_on = send_sample(a_next, 0, -1)
    a_far = send_sample(a_back, 0, 1)
    a_over_far = send_sample(a_over_back, 0, 1)
    b_far_over = send_sample(b_far, 1, 0)
    a_own, b_own = bring(after(a, a_over, b_back, b_on), b)
    parts = [a_own, a_back, a_on, a_far, a_over, a_over_back, a_over_on, a_over_far]
    parts += [b_own, b_back, b_on, b_far, b_over, b_back_over, b_on_over, b_far_over]
    where_a = [(i, 0) for i in range(8)]
    where_b = [(i, 0) for i in range(8, 16)]
    return parts, *[[(i, j * rows) for i, j in where] for where in (where_a, where_b)]


def column_steps(cols):
    return [pl.ds(first, CHUNK) for first in range(0, cols, CHUNK)]


def on_own(shape):
    row_ids = lax.broadcasted_iota(jnp.int32, shape, 0)
    return row_ids == lax.broadcasted_iota(jnp.int32, shape, 1)


def split_scalar(value, rows):
    wide = jnp.broadcast_to(value, (rows, LANES))
    high = wide.astype(BF16).astype(F32)
    lane = lax.broadcasted_iota(jnp.int32, wide.shape, 1)
    return jnp.where(lane < LANES // 2, high, (wide - high).astype(BF16).astype(F32))


def gram_kernel(core, *refs, where_a, where_b):
    vecs, keep, send, part_a, part_b = refs[-5:]
    count = (len(refs) - 5) // 2
    blocks, norms = refs[:count], refs[count : 2 * count]
    cols = vecs.shape[1]
    rows, total_rows = part_a.shape
    inv_rows = 1.0 / total_rows

    def view(where, part, columns, first_step):
        floats = jnp.concatenate([blocks[i][pl.ds(first, rows), columns] for i, first in where])
        floats = floats.astype(F32)
        mean = jnp.sum(floats, axis=0, keepdims=True) * inv_rows
        square = jnp.sum(floats * floats, axis=0, keepdims=True) * inv_rows
        scale = lax.rsqrt(square - mean * mean + EPSILON)
        norm = ((floats - mean) * scale).astype(BF16)
        for place, (i, first) in enumerate(where):
            norms[i][pl.ds(first, rows), columns] = norm[place * rows : (place + 1) * rows]
        more = lax.dot_general(
            norm[:rows], norm, (((1,), (1,)), ((), ())), preferred_element_type=F32
        )
        part[...] = more if first_step else part[...] + more
        return norm, scale

    loss = jnp.zeros((1, CHUNK), F32)
    for step, columns in enumerate(column_steps(cols)):
        norm_a, scale_a = view(where_a, part_a, columns, step == 0)
        norm_b, scale_b = view(where_b, part_b, columns, step == 0)
        diag = jnp.sum(norm_a.astype(F32) * norm_b.astype(F32), axis=0, keepdims=True) * inv_rows
        loss += (1.0 - diag) * (1.0 - diag) - OFF_WEIGHT * diag * diag
        slope = (diag - 1.0) - OFF_WEIGHT * diag
        vecs[:, columns] = jnp.concatenate([scale_a, scale_b, slope, jnp.zeros((5, CHUNK), F32)])

    shift = jnp.where(on_own(part_a.shape), 1.0 * cols, 0.0)
    gram_a = part_a[...] - shift
    gram_b = part_b[...] - shift
    keep[:, total_rows:] = split_scalar(jnp.sum(loss, axis=1, keepdims=True), rows)
    send[:, total_rows:] = jnp.zeros((rows, LANES), BF16)

    @pl.when(core[0] == 0)
    def _():
        keep[:, :total_rows] = gram_a
        send[:, :total_rows] = gram_b.astype(BF16)

    @pl.when(core[0] != 0)
    def _():
        keep[:, :total_rows] = gram_b
        send[:, :total_rows] = gram_a.astype(BF16)


def by_view(core, mine, theirs):
    first = core[0] == 0
    return jnp.where(first, mine[...], theirs[...]), jnp.where(first, theirs[...], mine[...])


def gradients(grams, blocks, vecs, columns, where_a, where_b, total_cols):
    gram_a, gram_b = grams
    rows, total_rows = gram_a.shape
    factor = OFF_WEIGHT / total_rows

    def view(where):
        return jnp.concatenate([blocks[i][pl.ds(first, rows), columns] for i, first in where])

    full_a, full_b = view(where_a), view(where_b)
    norm_a = full_a[:rows].astype(F32)
    norm_b = full_b[:rows].astype(F32)
    slope = vecs[2:3, columns]
    wide_a = jnp.dot(gram_b, full_a, preferred_element_type=F32)
    wide_b = jnp.dot(gram_a, full_b, preferred_element_type=F32)
    wide_a = factor * wide_a + factor * total_cols * norm_a + slope * norm_b
    wide_b = factor * wide_b + factor * total_cols * norm_b + slope * norm_a
    return norm_a, norm_b, wide_a, wide_b


def grad_kernel(core, mine, theirs, vecs, *refs, **layout):
    blocks, (high_a, low_a, high_b, low_b, stats) = refs[:-5], refs[-5:]
    cols = high_a.shape[1]
    grams = by_view(core, mine, theirs)
    back = jnp.where(on_own(mine.shape), 1.0 * layout["total_cols"], 0.0)
    square = (grams[0].astype(F32) + back) * (grams[1].astype(F32) + back)
    square = jnp.sum(jnp.sum(square, axis=0, keepdims=True), axis=1, keepdims=True)
    for columns in column_steps(cols):
        norm_a, norm_b, wide_a, wide_b = gradients(grams, blocks, vecs, columns, **layout)
        for wide, high, low in ((wide_a, high_a, low_a), (wide_b, high_b, low_b)):
            high[:, columns] = wide.astype(BF16)
            low[:, columns] = (wide - wide.astype(BF16).astype(F32)).astype(BF16)
        sums = [
            jnp.sum(wide_a, axis=0, keepdims=True),
            jnp.sum(wide_a * norm_a, axis=0, keepdims=True),
            jnp.sum(wide_b, axis=0, keepdims=True),
            jnp.sum(wide_b * norm_b, axis=0, keepdims=True),
        ]
        sums = jnp.concatenate(sums)
        for member in range(stats.shape[0]):
            stats[member, :, columns] = sums
    square = jnp.broadcast_to(square, (SUMS, LANES))
    for member in range(stats.shape[0]):
        stats[member, :, pl.ds(cols, LANES)] = square


def out_kernel(
    core,
    stats,
    high_a,
    low_a,
    high_b,
    low_b,
    own_a,
    own_b,
    vecs,
    split,
    other,
    grad_a,
    grad_b,
    loss,
    *,
    total_cols
):
    del core
    rows, cols = grad_a.shape
    members = stats.shape[0]
    inv_rows = 1.0 / (rows * members)
    sums = stats[0]
    for member in range(1, members):
        sums += stats[member]
    square = jnp.max(sums[0:1, cols:]) * (inv_rows * inv_rows)
    means = sums[:, :cols] * inv_rows
    norm_a = own_a[:rows, :].astype(F32)
    norm_b = own_b[:rows, :].astype(F32)
    wide_a = high_a[...].astype(F32) + low_a[...].astype(F32) - means[0:1] - norm_a * means[1:2]
    wide_b = high_b[...].astype(F32) + low_b[...].astype(F32) - means[2:3] - norm_b * means[3:4]
    grad_a[...] = (vecs[0:1, :] * wide_a).astype(BF16)
    grad_b[...] = (vecs[1:2, :] * wide_b).astype(BF16)
    diag = jnp.sum(split[0:1, :] + other[0:1, :]) * (2.0 / LANES)
    loss[0] = (diag + OFF_WEIGHT * square) / total_cols


def body(view_a, view_b):
    rows, cols = view_a.shape
    groups = lax.axis_size("sample")
    blocks = lax.axis_size("feat")
    chips = blocks // CORES
    total_rows = rows * groups
    core = (lax.axis_index("feat") & (CORES - 1)).reshape(1)
    shape = jax.ShapeDtypeStruct

    parts, where_a, where_b = gather_views(view_a, view_b)
    layout = dict(where_a=where_a, where_b=where_b)
    first = [where[0][0] for where in (where_a, where_b)]
    *norms, vecs, keep, send = call(
        functools.partial(gram_kernel, **layout),
        [core] + parts,
        [shape(part.shape, BF16) for part in parts]
        + [
            shape((8, cols), F32),
            shape((rows, total_rows + LANES), F32),
            shape((rows, total_rows + LANES), BF16),
        ],
        [pltpu.VMEM((rows, total_rows), F32)] * 2,
        aliases={i + 1: i for i in range(len(parts))},
        limit=16,
    )
    total = (keep + swap_cores(send).astype(F32)).astype(BF16)
    moved = exchange_chips(total)
    summed = jnp.sum(moved.reshape(chips, -1, moved.shape[1]).astype(F32), axis=0)
    split = summed[:8, total_rows:]
    sums = repeat_block(summed[:, :total_rows].astype(BF16), chips)
    sums, split = lax.optimization_barrier((sums, split))
    mine = exchange_chips(sums)
    theirs = swap_cores(mine)
    layout["total_cols"] = cols * blocks
    spare = [where_a[3][0], where_a[4][0], where_b[3][0], where_b[4][0]]
    *grads, stats = call(
        functools.partial(grad_kernel, **layout),
        [core, mine, theirs, vecs] + norms,
        [shape((rows, cols), BF16)] * 4 + [shape((groups, SUMS, cols + LANES), F32)],
        aliases={4 + index: i for i, index in enumerate(spare)},
        limit=8,
    )
    stats = lax.all_to_all(stats, "sample", split_axis=0, concat_axis=0, tiled=True)
    own = [norms[i] for i in first]
    grad_a, grad_b, loss = call(
        functools.partial(out_kernel, total_cols=cols * blocks),
        [core, stats] + grads + own + [vecs, split, swap_cores(split)],
        [shape((rows, cols), BF16), shape((rows, cols), BF16), shape((1,), F32)],
        limit=8,
    )
    return (loss.reshape(()), grad_a, grad_b)


def solution(mesh):
    in_specs = (P("sample", "feat"), P("sample", "feat"))
    out_specs = (P(), P("sample", "feat"), P("sample", "feat"))
    return jax.shard_map(body, mesh=mesh, in_specs=in_specs, out_specs=out_specs, check_vma=False)
```

```python
import functools
import jax
import jax.numpy as jnp
from jax import lax
from jax.experimental import pallas as pl
from jax.experimental.pallas import tpu as pltpu
from jax.sharding import PartitionSpec as P

EPSILON = 1e-05
OFF_WEIGHT = 0.0051
RING = 4
CORES = 2
F32 = jnp.float32
BF16 = jnp.bfloat16
LANES = 128
SUMS = 4
CHUNK = 512


def send_sample(block, turn, step):
    pairs = lax.axis_size("sample") // RING
    moves = [
        (z * RING + y, (z + turn) % pairs * RING + (y + step) % RING)
        for z in range(pairs)
        for y in range(RING)
    ]
    return lax.ppermute(block, "sample", moves)


def swap_cores(block):
    return lax.ppermute(block, "feat", [(i, i ^ 1) for i in range(lax.axis_size("feat"))])


def exchange_chips(block):
    members = lax.axis_size("feat") // CORES
    groups = [[i * CORES + core for i in range(members)] for core in range(CORES)]
    return lax.all_to_all(
        block, "feat", split_axis=0, concat_axis=0, tiled=True, axis_index_groups=groups
    )


def repeat_block(block, members):
    copies = jnp.broadcast_to(block[None], (members,) + block.shape)
    return copies.reshape((members * block.shape[0],) + block.shape[1:])


def call(kernel, args, outs, scratch=(), aliases=None, limit=16):
    def spec(shape):
        return pl.BlockSpec(memory_space=pltpu.SMEM if shape == (1,) else pltpu.VMEM)

    return pl.pallas_call(
        kernel,
        out_shape=outs,
        in_specs=[spec(arg.shape) for arg in args],
        out_specs=[spec(out.shape) for out in outs],
        scratch_shapes=list(scratch),
        input_output_aliases=aliases or {},
        compiler_params=pltpu.CompilerParams(vmem_limit_bytes=limit << 20),
    )(*args)


def bring_kernel(*refs):
    for source, place in zip(refs[: len(refs) // 2], refs[len(refs) // 2 :]):
        place[...] = source[...]


def bring(*blocks):
    return call(bring_kernel, blocks, [jax.ShapeDtypeStruct(x.shape, x.dtype) for x in blocks])


def after(block, *others):
    return lax.optimization_barrier((block,) + others)[0]


def gather_views(a, b):
    rows = a.shape[0]
    b_back = send_sample(b, 0, 1)
    b_on = send_sample(b, 0, -1)
    a_over = send_sample(a, 1, 0)
    a_next = after(a, b_back, b_on, a_over)
    b_far = send_sample(after(b_on, a_over, b_back), 0, -1)
    b_over = send_sample(after(b, a_over, b_back, b_on), 1, 0)
    b_back_over = send_sample(b_back, 1, 0)
    b_on_over = send_sample(b_on, 1, 0)
    a_over_back = send_sample(after(a_over, b_back, b_on), 0, 1)
    a_back = send_sample(a_next, 0, 1)
    a_over_on = send_sample(after(a_over, b_back, b_on), 0, -1)
    a_on = send_sample(a_next, 0, -1)
    a_far = send_sample(a_back, 0, 1)
    a_over_far = send_sample(a_over_back, 0, 1)
    b_far_over = send_sample(b_far, 1, 0)
    a_own, b_own = bring(after(a, a_over, b_back, b_on), b)
    parts = [a_own, a_back, a_on, a_far, a_over, a_over_back, a_over_on, a_over_far]
    parts += [b_own, b_back, b_on, b_far, b_over, b_back_over, b_on_over, b_far_over]
    where_a = [(i, 0) for i in range(8)]
    where_b = [(i, 0) for i in range(8, 16)]
    return parts, *[[(i, j * rows) for i, j in where] for where in (where_a, where_b)]


def column_steps(cols):
    return [pl.ds(first, CHUNK) for first in range(0, cols, CHUNK)]


def on_own(shape):
    row_ids = lax.broadcasted_iota(jnp.int32, shape, 0)
    return row_ids == lax.broadcasted_iota(jnp.int32, shape, 1)


def split_scalar(value, rows):
    wide = jnp.broadcast_to(value, (rows, LANES))
    high = wide.astype(BF16).astype(F32)
    lane = lax.broadcasted_iota(jnp.int32, wide.shape, 1)
    return jnp.where(lane < LANES // 2, high, (wide - high).astype(BF16).astype(F32))


def gram_kernel(core, *refs, where_a, where_b):
    vecs, keep, send, part_a, part_b = refs[-5:]
    count = (len(refs) - 5) // 2
    blocks, norms = refs[:count], refs[count : 2 * count]
    cols = vecs.shape[1]
    rows, total_rows = part_a.shape
    inv_rows = 1.0 / total_rows

    def fold(values):
        return jnp.sum(values.reshape(-1, 8, values.shape[1]), axis=0)

    def moments(where, columns):
        total = jnp.zeros((8, CHUNK), F32)
        square = jnp.zeros((8, CHUNK), F32)
        for i, first in where:
            floats = blocks[i][pl.ds(first, rows), columns].astype(F32)
            total += fold(floats)
            square += fold(floats * floats)
        mean = jnp.sum(total, axis=0, keepdims=True) * inv_rows
        square = jnp.sum(square, axis=0, keepdims=True) * inv_rows
        return mean, lax.rsqrt(square - mean * mean + EPSILON)

    def normal(i, first, columns, mean, scale):
        floats = blocks[i][pl.ds(first, rows), columns].astype(F32)
        norm = ((floats - mean) * scale).astype(BF16)
        norms[i][pl.ds(first, rows), columns] = norm
        return norm

    contract = (((1,), (1,)), ((), ()))
    loss = jnp.zeros((1, CHUNK), F32)
    for step, columns in enumerate(column_steps(cols)):
        mean_a, scale_a = moments(where_a, columns)
        mean_b, scale_b = moments(where_b, columns)
        diag = jnp.zeros((8, CHUNK), F32)
        for place in range(len(where_a)):
            norm_a = normal(*where_a[place], columns, mean_a, scale_a)
            norm_b = normal(*where_b[place], columns, mean_b, scale_b)
            diag += fold(norm_a.astype(F32) * norm_b.astype(F32))
            if place == 0:
                own_a, own_b = norm_a, norm_b
            part = pl.ds(place * rows, rows)
            more_a = lax.dot_general(own_a, norm_a, contract, preferred_element_type=F32)
            more_b = lax.dot_general(own_b, norm_b, contract, preferred_element_type=F32)
            part_a[:, part] = more_a if step == 0 else part_a[:, part] + more_a
            part_b[:, part] = more_b if step == 0 else part_b[:, part] + more_b
        diag = jnp.sum(diag, axis=0, keepdims=True) * inv_rows
        loss += (1.0 - diag) * (1.0 - diag) - OFF_WEIGHT * diag * diag
        slope = (diag - 1.0) - OFF_WEIGHT * diag
        vecs[:, columns] = jnp.concatenate([scale_a, scale_b, slope, jnp.zeros((5, CHUNK), F32)])

    shift = jnp.where(on_own(part_a.shape), 1.0 * cols, 0.0)
    gram_a = part_a[...] - shift
    gram_b = part_b[...] - shift
    keep[:, total_rows:] = split_scalar(jnp.sum(loss, axis=1, keepdims=True), rows)
    send[:, total_rows:] = jnp.zeros((rows, LANES), BF16)

    @pl.when(core[0] == 0)
    def _():
        keep[:, :total_rows] = gram_a
        send[:, :total_rows] = gram_b.astype(BF16)

    @pl.when(core[0] != 0)
    def _():
        keep[:, :total_rows] = gram_b
        send[:, :total_rows] = gram_a.astype(BF16)


def by_view(core, mine, theirs):
    first = core[0] == 0
    return jnp.where(first, mine[...], theirs[...]), jnp.where(first, theirs[...], mine[...])


def gradients(grams, blocks, vecs, columns, where_a, where_b, total_cols):
    gram_a, gram_b = grams
    rows, total_rows = gram_a.shape
    factor = OFF_WEIGHT / total_rows

    def view(where):
        return jnp.concatenate([blocks[i][pl.ds(first, rows), columns] for i, first in where])

    full_a, full_b = view(where_a), view(where_b)
    norm_a = full_a[:rows].astype(F32)
    norm_b = full_b[:rows].astype(F32)
    slope = vecs[2:3, columns]
    wide_a = jnp.dot(gram_b, full_a, preferred_element_type=F32)
    wide_b = jnp.dot(gram_a, full_b, preferred_element_type=F32)
    wide_a = factor * wide_a + factor * total_cols * norm_a + slope * norm_b
    wide_b = factor * wide_b + factor * total_cols * norm_b + slope * norm_a
    return norm_a, norm_b, wide_a, wide_b


def grad_kernel(core, mine, theirs, vecs, *refs, **layout):
    blocks, (high_a, low_a, high_b, low_b, stats) = refs[:-5], refs[-5:]
    cols = high_a.shape[1]
    grams = by_view(core, mine, theirs)
    back = jnp.where(on_own(mine.shape), 1.0 * layout["total_cols"], 0.0)
    square = (grams[0].astype(F32) + back) * (grams[1].astype(F32) + back)
    square = jnp.sum(jnp.sum(square, axis=0, keepdims=True), axis=1, keepdims=True)
    for columns in column_steps(cols):
        norm_a, norm_b, wide_a, wide_b = gradients(grams, blocks, vecs, columns, **layout)
        for wide, high, low in ((wide_a, high_a, low_a), (wide_b, high_b, low_b)):
            high[:, columns] = wide.astype(BF16)
            low[:, columns] = (wide - wide.astype(BF16).astype(F32)).astype(BF16)
        sums = [
            jnp.sum(wide_a, axis=0, keepdims=True),
            jnp.sum(wide_a * norm_a, axis=0, keepdims=True),
            jnp.sum(wide_b, axis=0, keepdims=True),
            jnp.sum(wide_b * norm_b, axis=0, keepdims=True),
        ]
        sums = jnp.concatenate(sums)
        for member in range(stats.shape[0]):
            stats[member, :, columns] = sums
    square = jnp.broadcast_to(square, (SUMS, LANES))
    for member in range(stats.shape[0]):
        stats[member, :, pl.ds(cols, LANES)] = square


def out_kernel(
    core,
    stats,
    high_a,
    low_a,
    high_b,
    low_b,
    own_a,
    own_b,
    vecs,
    split,
    other,
    grad_a,
    grad_b,
    loss,
    *,
    total_cols
):
    del core
    rows, cols = grad_a.shape
    members = stats.shape[0]
    inv_rows = 1.0 / (rows * members)
    sums = stats[0]
    for member in range(1, members):
        sums += stats[member]
    square = jnp.max(sums[0:1, cols:]) * (inv_rows * inv_rows)
    means = sums[:, :cols] * inv_rows
    norm_a = own_a[:rows, :].astype(F32)
    norm_b = own_b[:rows, :].astype(F32)
    wide_a = high_a[...].astype(F32) + low_a[...].astype(F32) - means[0:1] - norm_a * means[1:2]
    wide_b = high_b[...].astype(F32) + low_b[...].astype(F32) - means[2:3] - norm_b * means[3:4]
    grad_a[...] = (vecs[0:1, :] * wide_a).astype(BF16)
    grad_b[...] = (vecs[1:2, :] * wide_b).astype(BF16)
    diag = jnp.sum(split[0:1, :] + other[0:1, :]) * (2.0 / LANES)
    loss[0] = (diag + OFF_WEIGHT * square) / total_cols


def body(view_a, view_b):
    rows, cols = view_a.shape
    groups = lax.axis_size("sample")
    blocks = lax.axis_size("feat")
    chips = blocks // CORES
    total_rows = rows * groups
    core = (lax.axis_index("feat") & (CORES - 1)).reshape(1)
    shape = jax.ShapeDtypeStruct

    parts, where_a, where_b = gather_views(view_a, view_b)
    layout = dict(where_a=where_a, where_b=where_b)
    first = [where[0][0] for where in (where_a, where_b)]
    *norms, vecs, keep, send = call(
        functools.partial(gram_kernel, **layout),
        [core] + parts,
        [shape(part.shape, BF16) for part in parts]
        + [
            shape((8, cols), F32),
            shape((rows, total_rows + LANES), F32),
            shape((rows, total_rows + LANES), BF16),
        ],
        [pltpu.VMEM((rows, total_rows), F32)] * 2,
        aliases={i + 1: i for i in range(len(parts))},
        limit=16,
    )
    total = (keep + swap_cores(send).astype(F32)).astype(BF16)
    moved = exchange_chips(total)
    summed = jnp.sum(moved.reshape(chips, -1, moved.shape[1]).astype(F32), axis=0)
    split = summed[:8, total_rows:]
    sums = repeat_block(summed[:, :total_rows].astype(BF16), chips)
    sums, split = lax.optimization_barrier((sums, split))
    mine = exchange_chips(sums)
    theirs = swap_cores(mine)
    layout["total_cols"] = cols * blocks
    spare = [where_a[3][0], where_a[4][0], where_b[3][0], where_b[4][0]]
    *grads, stats = call(
        functools.partial(grad_kernel, **layout),
        [core, mine, theirs, vecs] + norms,
        [shape((rows, cols), BF16)] * 4 + [shape((groups, SUMS, cols + LANES), F32)],
        aliases={4 + index: i for i, index in enumerate(spare)},
        limit=8,
    )
    stats = lax.all_to_all(stats, "sample", split_axis=0, concat_axis=0, tiled=True)
    own = [norms[i] for i in first]
    grad_a, grad_b, loss = call(
        functools.partial(out_kernel, total_cols=cols * blocks),
        [core, stats] + grads + own + [vecs, split, swap_cores(split)],
        [shape((rows, cols), BF16), shape((rows, cols), BF16), shape((1,), F32)],
        limit=8,
    )
    return (loss.reshape(()), grad_a, grad_b)


def solution(mesh):
    in_specs = (P("sample", "feat"), P("sample", "feat"))
    out_specs = (P(), P("sample", "feat"), P("sample", "feat"))
    return jax.shard_map(body, mesh=mesh, in_specs=in_specs, out_specs=out_specs, check_vma=False)
```

```python
import functools
import jax
import jax.numpy as jnp
from jax import lax
from jax.experimental import pallas as pl
from jax.experimental.pallas import tpu as pltpu
from jax.sharding import PartitionSpec as P

EPSILON = 1e-05
OFF_WEIGHT = 0.0051
RING = 4
CORES = 2
F32 = jnp.float32
BF16 = jnp.bfloat16
LANES = 128
SUMS = 4
CHUNK = 512


def send_sample(block, turn, step):
    pairs = lax.axis_size("sample") // RING
    moves = [
        (z * RING + y, (z + turn) % pairs * RING + (y + step) % RING)
        for z in range(pairs)
        for y in range(RING)
    ]
    return lax.ppermute(block, "sample", moves)


def swap_cores(block):
    return lax.ppermute(block, "feat", [(i, i ^ 1) for i in range(lax.axis_size("feat"))])


def exchange_chips(block):
    members = lax.axis_size("feat") // CORES
    groups = [[i * CORES + core for i in range(members)] for core in range(CORES)]
    return lax.all_to_all(
        block, "feat", split_axis=0, concat_axis=0, tiled=True, axis_index_groups=groups
    )


def repeat_block(block, members):
    copies = jnp.broadcast_to(block[None], (members,) + block.shape)
    return copies.reshape((members * block.shape[0],) + block.shape[1:])


def call(kernel, args, outs, scratch=(), aliases=None, limit=16):
    def spec(shape):
        return pl.BlockSpec(memory_space=pltpu.SMEM if shape == (1,) else pltpu.VMEM)

    return pl.pallas_call(
        kernel,
        out_shape=outs,
        in_specs=[spec(arg.shape) for arg in args],
        out_specs=[spec(out.shape) for out in outs],
        scratch_shapes=list(scratch),
        input_output_aliases=aliases or {},
        compiler_params=pltpu.CompilerParams(vmem_limit_bytes=limit << 20),
    )(*args)


def bring_kernel(*refs):
    for source, place in zip(refs[: len(refs) // 2], refs[len(refs) // 2 :]):
        place[...] = source[...]


def bring(*blocks):
    return call(bring_kernel, blocks, [jax.ShapeDtypeStruct(x.shape, x.dtype) for x in blocks])


def after(block, *others):
    return lax.optimization_barrier((block,) + others)[0]


def gather_views(a, b):
    rows = a.shape[0]
    b_back = send_sample(b, 0, 1)
    b_on = send_sample(b, 0, -1)
    a_over = send_sample(a, 1, 0)
    a_next = after(a, b_back, b_on, a_over)
    b_far = send_sample(after(b_on, a_over, b_back), 0, -1)
    b_over = send_sample(after(b, a_over, b_back, b_on), 1, 0)
    b_back_over = send_sample(b_back, 1, 0)
    b_on_over = send_sample(b_on, 1, 0)
    a_over_back = send_sample(after(a_over, b_back, b_on), 0, 1)
    a_back = send_sample(a_next, 0, 1)
    a_over_on = send_sample(after(a_over, b_back, b_on), 0, -1)
    a_on = send_sample(a_next, 0, -1)
    a_far = send_sample(a_back, 0, 1)
    a_over_far = send_sample(a_over_back, 0, 1)
    b_far_over = send_sample(b_far, 1, 0)
    a_own, b_own = bring(after(a, a_over, b_back, b_on), b)
    parts = [a_own, a_back, a_on, a_far, a_over, a_over_back, a_over_on, a_over_far]
    parts += [b_own, b_back, b_on, b_far, b_over, b_back_over, b_on_over, b_far_over]
    where_a = [(i, 0) for i in range(8)]
    where_b = [(i, 0) for i in range(8, 16)]
    return parts, *[[(i, j * rows) for i, j in where] for where in (where_a, where_b)]


def column_steps(cols):
    return [pl.ds(first, CHUNK) for first in range(0, cols, CHUNK)]


def on_own(shape):
    row_ids = lax.broadcasted_iota(jnp.int32, shape, 0)
    return row_ids == lax.broadcasted_iota(jnp.int32, shape, 1)


def split_scalar(value, rows, half):
    wide = jnp.broadcast_to(value, (rows, LANES))
    high = wide.astype(BF16).astype(F32)
    low = (wide - high).astype(BF16).astype(F32)
    lane = lax.broadcasted_iota(jnp.int32, wide.shape, 1) - half * (LANES // 2)
    inside = (lane >= 0) & (lane < LANES // 2)
    return jnp.where(inside, jnp.where(lane < LANES // 4, high, low), 0.0)


def gram_kernel(core, *refs, where_a, where_b):
    vecs, keep, send, part_a, part_b = refs[-5:]
    count = (len(refs) - 5) // 2
    blocks, norms = refs[:count], refs[count : 2 * count]
    cols = vecs.shape[1]
    rows, total_rows = part_a.shape
    inv_rows = 1.0 / total_rows

    def fold(values):
        return jnp.sum(values.reshape(-1, 8, values.shape[1]), axis=0)

    def moments(where, columns):
        total = jnp.zeros((8, CHUNK), F32)
        square = jnp.zeros((8, CHUNK), F32)
        for i, first in where:
            floats = blocks[i][pl.ds(first, rows), columns].astype(F32)
            total += fold(floats)
            square += fold(floats * floats)
        mean = jnp.sum(total, axis=0, keepdims=True) * inv_rows
        square = jnp.sum(square, axis=0, keepdims=True) * inv_rows
        return mean, lax.rsqrt(square - mean * mean + EPSILON)

    def normal(i, first, columns, mean, scale):
        floats = blocks[i][pl.ds(first, rows), columns].astype(F32)
        norm = ((floats - mean) * scale).astype(BF16)
        norms[i][pl.ds(first, rows), columns] = norm
        return norm

    contract = (((1,), (1,)), ((), ()))
    loss = jnp.zeros((1, CHUNK), F32)
    for step, columns in enumerate(column_steps(cols)):
        mean_a, scale_a = moments(where_a, columns)
        mean_b, scale_b = moments(where_b, columns)
        diag = jnp.zeros((8, CHUNK), F32)
        for place in range(len(where_a)):
            norm_a = normal(*where_a[place], columns, mean_a, scale_a)
            norm_b = normal(*where_b[place], columns, mean_b, scale_b)
            diag += fold(norm_a.astype(F32) * norm_b.astype(F32))
            if place == 0:
                own_a, own_b = norm_a, norm_b
            part = pl.ds(place * rows, rows)
            more_a = lax.dot_general(own_a, norm_a, contract, preferred_element_type=F32)
            more_b = lax.dot_general(own_b, norm_b, contract, preferred_element_type=F32)
            part_a[:, part] = more_a if step == 0 else part_a[:, part] + more_a
            part_b[:, part] = more_b if step == 0 else part_b[:, part] + more_b
        diag = jnp.sum(diag, axis=0, keepdims=True) * inv_rows
        loss += (1.0 - diag) * (1.0 - diag) - OFF_WEIGHT * diag * diag
        slope = (diag - 1.0) - OFF_WEIGHT * diag
        vecs[:, columns] = jnp.concatenate([scale_a, scale_b, slope, jnp.zeros((5, CHUNK), F32)])

    shift = jnp.where(on_own(part_a.shape), 1.0 * cols, 0.0)
    gram_a = part_a[...] - shift
    gram_b = part_b[...] - shift
    loss = jnp.sum(loss, axis=1, keepdims=True)
    keep[:, total_rows:] = split_scalar(loss, rows, 0)
    send[:, total_rows:] = split_scalar(loss, rows, 1).astype(BF16)

    @pl.when(core[0] == 0)
    def _():
        keep[:, :total_rows] = gram_a
        send[:, :total_rows] = gram_b.astype(BF16)

    @pl.when(core[0] != 0)
    def _():
        keep[:, :total_rows] = gram_b
        send[:, :total_rows] = gram_a.astype(BF16)


def by_view(core, mine, theirs):
    first = core[0] == 0
    return jnp.where(first, mine[...], theirs[...]), jnp.where(first, theirs[...], mine[...])


def gradients(grams, blocks, vecs, columns, where_a, where_b, total_cols):
    gram_a, gram_b = grams
    rows, total_rows = gram_a.shape
    factor = OFF_WEIGHT / total_rows

    def view(where):
        return jnp.concatenate([blocks[i][pl.ds(first, rows), columns] for i, first in where])

    full_a, full_b = view(where_a), view(where_b)
    norm_a = full_a[:rows].astype(F32)
    norm_b = full_b[:rows].astype(F32)
    slope = vecs[2:3, columns]
    wide_a = jnp.dot(gram_b, full_a, preferred_element_type=F32)
    wide_b = jnp.dot(gram_a, full_b, preferred_element_type=F32)
    wide_a = factor * wide_a + factor * total_cols * norm_a + slope * norm_b
    wide_b = factor * wide_b + factor * total_cols * norm_b + slope * norm_a
    return norm_a, norm_b, wide_a, wide_b


def grad_kernel(core, mine, theirs, vecs, *refs, **layout):
    blocks, (high_a, low_a, high_b, low_b, stats) = refs[:-5], refs[-5:]
    cols = high_a.shape[1]
    grams = by_view(core, mine, theirs)
    back = jnp.where(on_own(mine.shape), 1.0 * layout["total_cols"], 0.0)
    square = (grams[0].astype(F32) + back) * (grams[1].astype(F32) + back)
    square = jnp.sum(jnp.sum(square, axis=0, keepdims=True), axis=1, keepdims=True)
    for columns in column_steps(cols):
        norm_a, norm_b, wide_a, wide_b = gradients(grams, blocks, vecs, columns, **layout)
        for wide, high, low in ((wide_a, high_a, low_a), (wide_b, high_b, low_b)):
            high[:, columns] = wide.astype(BF16)
            low[:, columns] = (wide - wide.astype(BF16).astype(F32)).astype(BF16)
        sums = [
            jnp.sum(wide_a, axis=0, keepdims=True),
            jnp.sum(wide_a * norm_a, axis=0, keepdims=True),
            jnp.sum(wide_b, axis=0, keepdims=True),
            jnp.sum(wide_b * norm_b, axis=0, keepdims=True),
        ]
        sums = jnp.concatenate(sums)
        for member in range(stats.shape[0]):
            stats[member, :, columns] = sums
    square = jnp.broadcast_to(square, (SUMS, LANES))
    for member in range(stats.shape[0]):
        stats[member, :, pl.ds(cols, LANES)] = square


def out_kernel(
    core,
    stats,
    high_a,
    low_a,
    high_b,
    low_b,
    own_a,
    own_b,
    vecs,
    split,
    grad_a,
    grad_b,
    loss,
    *,
    total_cols
):
    del core
    rows, cols = grad_a.shape
    members = stats.shape[0]
    inv_rows = 1.0 / (rows * members)
    sums = stats[0]
    for member in range(1, members):
        sums += stats[member]
    square = jnp.max(sums[0:1, cols:]) * (inv_rows * inv_rows)
    means = sums[:, :cols] * inv_rows
    norm_a = own_a[:rows, :].astype(F32)
    norm_b = own_b[:rows, :].astype(F32)
    wide_a = high_a[...].astype(F32) + low_a[...].astype(F32) - means[0:1] - norm_a * means[1:2]
    wide_b = high_b[...].astype(F32) + low_b[...].astype(F32) - means[2:3] - norm_b * means[3:4]
    grad_a[...] = (vecs[0:1, :] * wide_a).astype(BF16)
    grad_b[...] = (vecs[1:2, :] * wide_b).astype(BF16)
    diag = jnp.sum(split[0:1, :]) * (4.0 / LANES)
    loss[0] = (diag + OFF_WEIGHT * square) / total_cols


def body(view_a, view_b):
    rows, cols = view_a.shape
    groups = lax.axis_size("sample")
    blocks = lax.axis_size("feat")
    chips = blocks // CORES
    total_rows = rows * groups
    core = (lax.axis_index("feat") & (CORES - 1)).reshape(1)
    shape = jax.ShapeDtypeStruct

    parts, where_a, where_b = gather_views(view_a, view_b)
    layout = dict(where_a=where_a, where_b=where_b)
    first = [where[0][0] for where in (where_a, where_b)]
    *norms, vecs, keep, send = call(
        functools.partial(gram_kernel, **layout),
        [core] + parts,
        [shape(part.shape, BF16) for part in parts]
        + [
            shape((8, cols), F32),
            shape((rows, total_rows + LANES), F32),
            shape((rows, total_rows + LANES), BF16),
        ],
        [pltpu.VMEM((rows, total_rows), F32)] * 2,
        aliases={i + 1: i for i in range(len(parts))},
        limit=16,
    )
    total = (keep + swap_cores(send).astype(F32)).astype(BF16)
    moved = exchange_chips(total)
    summed = jnp.sum(moved.reshape(chips, -1, moved.shape[1]).astype(F32), axis=0)
    split = summed[:8, total_rows:]
    sums = repeat_block(summed[:, :total_rows].astype(BF16), chips)
    sums, split = lax.optimization_barrier((sums, split))
    mine = exchange_chips(sums)
    theirs = swap_cores(mine)
    layout["total_cols"] = cols * blocks
    spare = [where_a[3][0], where_a[4][0], where_b[3][0], where_b[4][0]]
    *grads, stats = call(
        functools.partial(grad_kernel, **layout),
        [core, mine, theirs, vecs] + norms,
        [shape((rows, cols), BF16)] * 4 + [shape((groups, SUMS, cols + LANES), F32)],
        aliases={4 + index: i for i, index in enumerate(spare)},
        limit=8,
    )
    stats = lax.all_to_all(stats, "sample", split_axis=0, concat_axis=0, tiled=True)
    own = [norms[i] for i in first]
    grad_a, grad_b, loss = call(
        functools.partial(out_kernel, total_cols=cols * blocks),
        [core, stats] + grads + own + [vecs, split],
        [shape((rows, cols), BF16), shape((rows, cols), BF16), shape((1,), F32)],
        limit=8,
    )
    return (loss.reshape(()), grad_a, grad_b)


def solution(mesh):
    in_specs = (P("sample", "feat"), P("sample", "feat"))
    out_specs = (P(), P("sample", "feat"), P("sample", "feat"))
    return jax.shard_map(body, mesh=mesh, in_specs=in_specs, out_specs=out_specs, check_vma=False)
```

```python
import functools
import jax
import jax.numpy as jnp
from jax import lax
from jax.experimental import pallas as pl
from jax.experimental.pallas import tpu as pltpu
from jax.sharding import PartitionSpec as P

EPSILON = 1e-05
OFF_WEIGHT = 0.0051
RING = 4
CORES = 2
F32 = jnp.float32
BF16 = jnp.bfloat16
LANES = 128
SUMS = 4
CHUNK = 256


def send_sample(block, turn, step):
    pairs = lax.axis_size("sample") // RING
    moves = [
        (z * RING + y, (z + turn) % pairs * RING + (y + step) % RING)
        for z in range(pairs)
        for y in range(RING)
    ]
    return lax.ppermute(block, "sample", moves)


def swap_cores(block):
    return lax.ppermute(block, "feat", [(i, i ^ 1) for i in range(lax.axis_size("feat"))])


def exchange_chips(block):
    members = lax.axis_size("feat") // CORES
    groups = [[i * CORES + core for i in range(members)] for core in range(CORES)]
    return lax.all_to_all(
        block, "feat", split_axis=0, concat_axis=0, tiled=True, axis_index_groups=groups
    )


def repeat_block(block, members):
    copies = jnp.broadcast_to(block[None], (members,) + block.shape)
    return copies.reshape((members * block.shape[0],) + block.shape[1:])


def call(kernel, args, outs, scratch=(), aliases=None, limit=16):
    def spec(shape):
        return pl.BlockSpec(memory_space=pltpu.SMEM if shape == (1,) else pltpu.VMEM)

    return pl.pallas_call(
        kernel,
        out_shape=outs,
        in_specs=[spec(arg.shape) for arg in args],
        out_specs=[spec(out.shape) for out in outs],
        scratch_shapes=list(scratch),
        input_output_aliases=aliases or {},
        compiler_params=pltpu.CompilerParams(vmem_limit_bytes=limit << 20),
    )(*args)


def bring_kernel(*refs):
    for source, place in zip(refs[: len(refs) // 2], refs[len(refs) // 2 :]):
        place[...] = source[...]


def bring(*blocks):
    return call(bring_kernel, blocks, [jax.ShapeDtypeStruct(x.shape, x.dtype) for x in blocks])


def after(block, *others):
    return lax.optimization_barrier((block,) + others)[0]


def gather_views(a, b):
    rows = a.shape[0]
    b_back = send_sample(b, 0, 1)
    b_on = send_sample(b, 0, -1)
    a_over = send_sample(a, 1, 0)
    a_next = after(a, b_back, b_on, a_over)
    b_far = send_sample(after(b_on, b_back), 0, -1)
    b_over = send_sample(after(b, a_over), 1, 0)
    b_back_over = send_sample(b_back, 1, 0)
    b_on_over = send_sample(b_on, 1, 0)
    a_over_back = send_sample(after(a_over, b_back, b_on), 0, 1)
    a_back = send_sample(a_next, 0, 1)
    a_over_on = send_sample(after(a_over, b_back, b_on), 0, -1)
    a_on = send_sample(a_next, 0, -1)
    a_far = send_sample(a_back, 0, 1)
    a_over_far = send_sample(a_over_back, 0, 1)
    b_far_over = send_sample(b_far, 1, 0)
    a_own, b_own = bring(after(a, a_back), after(b, a_back))
    parts = [a_own, a_back, a_on, a_far, a_over, a_over_back, a_over_on, a_over_far]
    parts += [b_own, b_back, b_on, b_far, b_over, b_back_over, b_on_over, b_far_over]
    where_a = [(i, 0) for i in range(8)]
    where_b = [(i, 0) for i in range(8, 16)]
    return parts, *[[(i, j * rows) for i, j in where] for where in (where_a, where_b)]


def column_steps(cols):
    return [pl.ds(first, CHUNK) for first in range(0, cols, CHUNK)]


def on_own(shape):
    row_ids = lax.broadcasted_iota(jnp.int32, shape, 0)
    return row_ids == lax.broadcasted_iota(jnp.int32, shape, 1)


def split_scalar(value, rows, half):
    wide = jnp.broadcast_to(value, (rows, LANES))
    high = wide.astype(BF16).astype(F32)
    low = (wide - high).astype(BF16).astype(F32)
    lane = lax.broadcasted_iota(jnp.int32, wide.shape, 1) - half * (LANES // 2)
    inside = (lane >= 0) & (lane < LANES // 2)
    return jnp.where(inside, jnp.where(lane < LANES // 4, high, low), 0.0)


def gram_kernel(core, *refs, where_a, where_b):
    vecs, keep, send, part_a, part_b = refs[-5:]
    count = (len(refs) - 5) // 2
    blocks, norms = refs[:count], refs[count : 2 * count]
    cols = vecs.shape[1]
    rows, total_rows = part_a.shape
    inv_rows = 1.0 / total_rows

    def fold(values):
        return jnp.sum(values.reshape(-1, 8, values.shape[1]), axis=0)

    def moments(where, columns):
        total = jnp.zeros((8, CHUNK), F32)
        square = jnp.zeros((8, CHUNK), F32)
        for i, first in where:
            floats = blocks[i][pl.ds(first, rows), columns].astype(F32)
            total += fold(floats)
            square += fold(floats * floats)
        mean = jnp.sum(total, axis=0, keepdims=True) * inv_rows
        square = jnp.sum(square, axis=0, keepdims=True) * inv_rows
        return mean, lax.rsqrt(square - mean * mean + EPSILON)

    def normal(i, first, columns, mean, scale):
        floats = blocks[i][pl.ds(first, rows), columns].astype(F32)
        norm = ((floats - mean) * scale).astype(BF16)
        norms[i][pl.ds(first, rows), columns] = norm
        return norm

    contract = (((1,), (1,)), ((), ()))
    loss = jnp.zeros((1, CHUNK), F32)
    for step, columns in enumerate(column_steps(cols)):
        mean_a, scale_a = moments(where_a, columns)
        mean_b, scale_b = moments(where_b, columns)
        diag = jnp.zeros((8, CHUNK), F32)
        for place in range(len(where_a)):
            norm_a = normal(*where_a[place], columns, mean_a, scale_a)
            norm_b = normal(*where_b[place], columns, mean_b, scale_b)
            diag += fold(norm_a.astype(F32) * norm_b.astype(F32))
            if place == 0:
                own_a, own_b = norm_a, norm_b
            part = pl.ds(place * rows, rows)
            more_a = lax.dot_general(own_a, norm_a, contract, preferred_element_type=F32)
            more_b = lax.dot_general(own_b, norm_b, contract, preferred_element_type=F32)
            part_a[:, part] = more_a if step == 0 else part_a[:, part] + more_a
            part_b[:, part] = more_b if step == 0 else part_b[:, part] + more_b
        diag = jnp.sum(diag, axis=0, keepdims=True) * inv_rows
        loss += (1.0 - diag) * (1.0 - diag) - OFF_WEIGHT * diag * diag
        slope = (diag - 1.0) - OFF_WEIGHT * diag
        vecs[:, columns] = jnp.concatenate([scale_a, scale_b, slope, jnp.zeros((5, CHUNK), F32)])

    shift = jnp.where(on_own(part_a.shape), 1.0 * cols, 0.0)
    gram_a = part_a[...] - shift
    gram_b = part_b[...] - shift
    loss = jnp.sum(loss, axis=1, keepdims=True)
    keep[:, total_rows:] = split_scalar(loss, rows, 0)
    send[:, total_rows:] = split_scalar(loss, rows, 1).astype(BF16)

    @pl.when(core[0] == 0)
    def _():
        keep[:, :total_rows] = gram_a
        send[:, :total_rows] = gram_b.astype(BF16)

    @pl.when(core[0] != 0)
    def _():
        keep[:, :total_rows] = gram_b
        send[:, :total_rows] = gram_a.astype(BF16)


def by_view(core, mine, theirs):
    first = core[0] == 0
    return jnp.where(first, mine[...], theirs[...]), jnp.where(first, theirs[...], mine[...])


def gradients(grams, blocks, vecs, columns, where_a, where_b, total_cols):
    gram_a, gram_b = grams
    rows, total_rows = gram_a.shape
    factor = OFF_WEIGHT / total_rows

    def view(where):
        return jnp.concatenate([blocks[i][pl.ds(first, rows), columns] for i, first in where])

    full_a, full_b = view(where_a), view(where_b)
    norm_a = full_a[:rows].astype(F32)
    norm_b = full_b[:rows].astype(F32)
    slope = vecs[2:3, columns]
    wide_a = jnp.dot(gram_b, full_a, preferred_element_type=F32)
    wide_b = jnp.dot(gram_a, full_b, preferred_element_type=F32)
    wide_a = factor * wide_a + factor * total_cols * norm_a + slope * norm_b
    wide_b = factor * wide_b + factor * total_cols * norm_b + slope * norm_a
    return norm_a, norm_b, wide_a, wide_b


def grad_kernel(core, mine, theirs, vecs, *refs, **layout):
    blocks, (high_a, low_a, high_b, low_b, stats) = refs[:-5], refs[-5:]
    cols = high_a.shape[1]
    grams = by_view(core, mine, theirs)
    back = jnp.where(on_own(mine.shape), 1.0 * layout["total_cols"], 0.0)
    square = (grams[0].astype(F32) + back) * (grams[1].astype(F32) + back)
    square = jnp.sum(jnp.sum(square, axis=0, keepdims=True), axis=1, keepdims=True)
    for columns in column_steps(cols):
        norm_a, norm_b, wide_a, wide_b = gradients(grams, blocks, vecs, columns, **layout)
        for wide, high, low in ((wide_a, high_a, low_a), (wide_b, high_b, low_b)):
            high[:, columns] = wide.astype(BF16)
            low[:, columns] = (wide - wide.astype(BF16).astype(F32)).astype(BF16)
        sums = [
            jnp.sum(wide_a, axis=0, keepdims=True),
            jnp.sum(wide_a * norm_a, axis=0, keepdims=True),
            jnp.sum(wide_b, axis=0, keepdims=True),
            jnp.sum(wide_b * norm_b, axis=0, keepdims=True),
        ]
        sums = jnp.concatenate(sums)
        for member in range(stats.shape[0]):
            stats[member, :, columns] = sums
    square = jnp.broadcast_to(square, (SUMS, LANES))
    for member in range(stats.shape[0]):
        stats[member, :, pl.ds(cols, LANES)] = square


def out_kernel(
    core,
    stats,
    high_a,
    low_a,
    high_b,
    low_b,
    own_a,
    own_b,
    vecs,
    split,
    grad_a,
    grad_b,
    loss,
    *,
    total_cols
):
    del core
    rows, cols = grad_a.shape
    members = stats.shape[0]
    inv_rows = 1.0 / (rows * members)
    sums = stats[0]
    for member in range(1, members):
        sums += stats[member]
    square = jnp.max(sums[0:1, cols:]) * (inv_rows * inv_rows)
    means = sums[:, :cols] * inv_rows
    norm_a = own_a[:rows, :].astype(F32)
    norm_b = own_b[:rows, :].astype(F32)
    wide_a = high_a[...].astype(F32) + low_a[...].astype(F32) - means[0:1] - norm_a * means[1:2]
    wide_b = high_b[...].astype(F32) + low_b[...].astype(F32) - means[2:3] - norm_b * means[3:4]
    grad_a[...] = (vecs[0:1, :] * wide_a).astype(BF16)
    grad_b[...] = (vecs[1:2, :] * wide_b).astype(BF16)
    diag = jnp.sum(split[0:1, :]) * (4.0 / LANES)
    loss[0] = (diag + OFF_WEIGHT * square) / total_cols


def body(view_a, view_b):
    rows, cols = view_a.shape
    groups = lax.axis_size("sample")
    blocks = lax.axis_size("feat")
    chips = blocks // CORES
    total_rows = rows * groups
    core = (lax.axis_index("feat") & (CORES - 1)).reshape(1)
    shape = jax.ShapeDtypeStruct

    parts, where_a, where_b = gather_views(view_a, view_b)
    layout = dict(where_a=where_a, where_b=where_b)
    first = [where[0][0] for where in (where_a, where_b)]
    *norms, vecs, keep, send = call(
        functools.partial(gram_kernel, **layout),
        [core] + parts,
        [shape(part.shape, BF16) for part in parts]
        + [
            shape((8, cols), F32),
            shape((rows, total_rows + LANES), F32),
            shape((rows, total_rows + LANES), BF16),
        ],
        [pltpu.VMEM((rows, total_rows), F32)] * 2,
        aliases={i + 1: i for i in range(len(parts))},
        limit=16,
    )
    total = (keep + swap_cores(send).astype(F32)).astype(BF16)
    moved = exchange_chips(total)
    summed = jnp.sum(moved.reshape(chips, -1, moved.shape[1]).astype(F32), axis=0)
    split = summed[:8, total_rows:]
    sums = repeat_block(summed[:, :total_rows].astype(BF16), chips)
    sums, split = lax.optimization_barrier((sums, split))
    mine = exchange_chips(sums)
    theirs = swap_cores(mine)
    layout["total_cols"] = cols * blocks
    spare = [where_a[3][0], where_a[4][0], where_b[3][0], where_b[4][0]]
    *grads, stats = call(
        functools.partial(grad_kernel, **layout),
        [core, mine, theirs, vecs] + norms,
        [shape((rows, cols), BF16)] * 4 + [shape((groups, SUMS, cols + LANES), F32)],
        aliases={4 + index: i for i, index in enumerate(spare)},
        limit=8,
    )
    stats = lax.all_to_all(stats, "sample", split_axis=0, concat_axis=0, tiled=True)
    own = [norms[i] for i in first]
    grad_a, grad_b, loss = call(
        functools.partial(out_kernel, total_cols=cols * blocks),
        [core, stats] + grads + own + [vecs, split],
        [shape((rows, cols), BF16), shape((rows, cols), BF16), shape((1,), F32)],
        limit=8,
    )
    return (loss.reshape(()), grad_a, grad_b)


def solution(mesh):
    in_specs = (P("sample", "feat"), P("sample", "feat"))
    out_specs = (P(), P("sample", "feat"), P("sample", "feat"))
    return jax.shard_map(body, mesh=mesh, in_specs=in_specs, out_specs=out_specs, check_vma=False)
```
